32 devices in a mesh: wide: 8 (over z, y), lev: 4 (over x, core).
Axes of the slice: x: 2, y: 2, z: 4, core: 2. Of those that a mesh axis runs over, the one named last changes fastest.
Arguments:
- state_field: float32 [12, 1472, 1472], P('lev', 'wide'), may hold values from -8 to 8
- to_modes: float32 [12, 12], replicated, may hold values from -4 to 4
- from_modes: float32 [12, 12], replicated, may hold values from -4 to 4, as said below
- mode_depth: float32 [12], replicated, may hold values from 0.1 to 2000
Outputs:
- updated_field: float32 [12, 1472, 1472], P('lev', 'wide')
The draws below stay inside these ranges and needn't reach their ends.
Inputs may be any that keep to these rules, and one draw needn't show every extreme that they name: `from_modes`: the inverse of to_modes.
All inputs are finite; a program needn't handle non-finite values.
Results may differ from the reference program's by a relative error of at most 0.000094.
Values sent between devices are 32-bit elements; how exact they have to be, the bound alone decides.
No kernel may reach another device: no remote copies, remote signals or barrier semaphores. Data moves between devices by JAX's collectives and lax.ppermute only.
A program may use at most 64 MiB of HBM per device.

```python
import math
import jax
import jax.numpy as jnp
from jax import lax

I = 1472
E = 64
K = 12
KT = 512


def mode_pair(key):
    noise = jax.random.truncated_normal(key, -3.0, 3.0, (K, K), jnp.float32)
    return jnp.eye(K, dtype=jnp.float32) + 0.25 / math.sqrt(K) * noise


def draw_to_modes(key, part):
    return mode_pair(jax.random.fold_in(key, 11))


def draw_from_modes(key, part):
    return jnp.linalg.inv(mode_pair(jax.random.fold_in(key, 11)))


def draw_state_field(key, part):
    first_key = jax.random.fold_in(jax.random.fold_in(key, 5), 0)
    return jax.random.truncated_normal(first_key, -6.0, 6.0, (K, I, I), jnp.float32)


def setup_inputs(seed: int = 0) -> dict:
    key_list = jax.random.split(jax.random.key(seed), 5)
    return {
        "state_field": draw_state_field(jax.random.fold_in(key_list[4], 71), 0),
        "to_modes": draw_to_modes(jax.random.fold_in(key_list[4], 71), 0),
        "from_modes": draw_from_modes(jax.random.fold_in(key_list[4], 71), 0),
        "mode_depth": jnp.clip(jnp.exp(jax.random.uniform(key_list[3], (K,), jnp.float32, math.log(0.1), math.log(2000.0))), 0.1, 2000.0),
    }


def blend_weights(fraction):
    square = fraction * fraction
    cubed = square * fraction
    return (2.0 * cubed - 3.0 * square + 1.0, cubed - 2.0 * square + fraction, -2.0 * cubed + 3.0 * square, cubed - square)

def hermite_mix(start_val, start_slope, end_val, end_slope, weights):
    return weights[0] * end_val + weights[1] * end_slope + weights[2] * start_val + weights[3] * start_slope

def extend_cols(sub_block, extra):
    fraction = (jnp.arange(extra, dtype=jnp.float32) + 1.0) / (extra + 1.0)
    weights = blend_weights(fraction)
    end_val = sub_block[..., -1:]
    end_slope = sub_block[..., -1:] - sub_block[..., -2:-1]
    start_val = sub_block[..., :1]
    start_slope = sub_block[..., 1:2] - sub_block[..., :1]
    added = hermite_mix(start_val, start_slope, end_val, end_slope, weights)
    return jnp.concatenate([sub_block, added], axis=-1)

def laplace(waves, length):
    sines = jnp.sin(math.pi / length * waves.astype(jnp.float32))
    return 4.0 * sines * sines

def hartley(values, axis):
    spectral = jnp.fft.fft(values, axis=axis)
    return jnp.real(spectral) - jnp.imag(spectral)

def reference(state_field, to_modes, from_modes, mode_depth):
    length = I + E

    def forward(one_level):
        tall = jnp.swapaxes(extend_cols(jnp.swapaxes(one_level, 0, 1), E), 0, 1)
        extended = extend_cols(tall, E)
        return hartley(hartley(extended, 0), 1)
    spectra = lax.map(forward, state_field)
    indices = jnp.arange(length, dtype=jnp.int32)
    magnitude = jnp.minimum(indices, length - indices)
    lap_line = laplace(indices, length)
    inside = magnitude[:, None] * magnitude[:, None] + magnitude[None, :] * magnitude[None, :] < KT * KT
    keep_mask = inside.astype(jnp.float32)
    lap_sum = lap_line[:, None] + lap_line[None, :]
    mode_values = jnp.einsum('ml,lyx->myx', to_modes, spectra, precision=lax.Precision.HIGHEST)
    solved = mode_values * keep_mask / (1.0 + mode_depth[:, None, None] * lap_sum)
    mixed_levels = jnp.einsum('lm,myx->lyx', from_modes, solved, precision=lax.Precision.HIGHEST)

    def inverse(one_level):
        return (hartley(hartley(one_level, 0), 1) / (length * length))[:I, :I]
    return lax.map(inverse, mixed_levels)
```

```python
import math

import jax
import jax.numpy as jnp
import numpy as np
from jax import lax
from jax.sharding import PartitionSpec as P

I = 1472
E = 64
KT = 512
STEP = 16

HIGH = lax.Precision.HIGH
HIGHEST = lax.Precision.HIGHEST
AXES = ("wide", "lev")


def blend_weights(extra):
    f = (np.arange(extra, dtype=np.float64) + 1.0) / (extra + 1.0)
    f2, f3 = f * f, f * f * f
    return 2 * f3 - 3 * f2 + 1, f3 - 2 * f2 + f, -2 * f3 + 3 * f2, f3 - f2


def edge_weights(extra):
    h00, h10, h01, h11 = blend_weights(extra)
    return np.stack([h01 - h11, h11, -h10, h00 + h10]).astype(np.float32)


def extend(block, extra):
    w = jnp.asarray(edge_weights(extra))
    added = (
        block[..., :1] * w[0] + block[..., 1:2] * w[1] + block[..., -2:-1] * w[2] + block[..., -1:] * w[3]
    )
    return jnp.concatenate([block, added], axis=-1)


def cas_seeds(waves, positions, length):
    turn = 2.0 * np.pi / length
    base = waves[::STEP].astype(np.int64)
    coarse = turn * ((base[:, None] * positions[None, :]) % length)
    fine = turn * ((np.arange(STEP)[:, None] * positions[None, :]) % length)
    parts = np.cos(coarse) + np.sin(coarse), np.cos(coarse) - np.sin(coarse), np.cos(fine), np.sin(fine)
    return [np.asarray(a, np.float32) for a in parts]


def cas_table(waves, positions, length):
    plus, minus, cosine, sine = (jnp.asarray(a) for a in cas_seeds(waves, positions, length))
    table = plus[:, None, :] * cosine[None] + minus[:, None, :] * sine[None]
    return table.reshape(len(waves), len(positions))


def plain(state, to_modes, from_modes, mode_depth):
    wide, lev = lax.axis_size("wide"), lax.axis_size("lev")
    devices = wide * lev
    levels, rows, cols = state.shape
    length = I + E
    waves = np.arange(-KT, KT)
    share = len(waves) // devices
    table = cas_table(waves, np.arange(length), length)
    spec = jnp.einsum("qn,lrn->qlr", table, extend(state, E), precision=HIGH)
    spec = spec.reshape(devices, share, levels * rows)
    spec = lax.all_to_all(spec, AXES, 0, 0, tiled=True)
    spec = spec.reshape(wide, lev, share, levels, rows).transpose(1, 3, 2, 0, 4)
    spec = extend(spec.reshape(lev * levels, share, wide * rows), E)
    spec = jnp.einsum("lqr,pr->lqp", spec, table, precision=HIGH)
    first = (lax.axis_index("wide") * lev + lax.axis_index("lev")) * share
    lap = (4.0 * np.sin(np.pi * waves / length) ** 2).astype(np.float32)
    square = (waves * waves).astype(np.int32)
    lap_q = lax.dynamic_slice_in_dim(jnp.asarray(lap), first, share)
    square_q = lax.dynamic_slice_in_dim(jnp.asarray(square), first, share)
    keep = (square_q[:, None] + square[None, :] < KT * KT).astype(jnp.float32)
    modes = jnp.einsum("ml,lqp->mqp", to_modes, spec, precision=HIGHEST)
    solved = modes * keep / (1.0 + mode_depth[:, None, None] * (lap_q[:, None] + lap[None, :]))
    mixed = jnp.einsum("lm,mqp->lqp", from_modes, solved, precision=HIGHEST)
    back = jnp.einsum("lqp,pr->lqr", mixed, table[:, :I], precision=HIGH)
    back = back.reshape(lev, levels, share, wide, rows).transpose(3, 0, 2, 1, 4)
    back = lax.all_to_all(back.reshape(devices, share, levels * rows), AXES, 0, 0, tiled=True)
    back = back.reshape(len(waves), levels, rows)
    return jnp.einsum("qlr,qn->lrn", back, table[:, :I], precision=HIGH) / (length * length)


def solution(mesh):
    placed = (P("lev", "wide", None), P(), P(), P())
    return jax.shard_map(
        plain, mesh=mesh, in_specs=placed, out_specs=P("lev", "wide", None), check_vma=False
    )
```

```python
import functools

import jax
import jax.numpy as jnp
import numpy as np
from jax import lax
from jax.experimental import pallas as pl
from jax.experimental.pallas import tpu as pltpu
from jax.sharding import PartitionSpec as P

I = 1472
E = 64
KT = 512
STEP = 16
LANES = 128
HALF = 64
TILE = 256

HIGH = lax.Precision.HIGH
HIGHEST = lax.Precision.HIGHEST
AXES = ("wide", "lev")


def blend_weights(extra):
    f = (np.arange(extra, dtype=np.float64) + 1.0) / (extra + 1.0)
    f2, f3 = f * f, f * f * f
    return 2 * f3 - 3 * f2 + 1, f3 - 2 * f2 + f, -2 * f3 + 3 * f2, f3 - f2


def edge_weights(extra):
    h00, h10, h01, h11 = blend_weights(extra)
    return np.stack([h01 - h11, h11, -h10, h00 + h10]).astype(np.float32)


def extend(block, extra):
    w = jnp.asarray(edge_weights(extra))
    added = (
        block[..., :1] * w[0] + block[..., 1:2] * w[1] + block[..., -2:-1] * w[2] + block[..., -1:] * w[3]
    )
    return jnp.concatenate([block, added], axis=-1)


def cas_seeds(waves, positions, length):
    turn = 2.0 * np.pi / length
    base = waves[::STEP].astype(np.int64)
    coarse = turn * ((base[:, None] * positions[None, :]) % length)
    fine = turn * ((np.arange(STEP)[:, None] * positions[None, :]) % length)
    parts = np.cos(coarse) + np.sin(coarse), np.cos(coarse) - np.sin(coarse), np.cos(fine), np.sin(fine)
    return [np.asarray(a, np.float32) for a in parts]


def cas_table(waves, positions, length):
    plus, minus, cosine, sine = (jnp.asarray(a) for a in cas_seeds(waves, positions, length))
    table = plus[:, None, :] * cosine[None] + minus[:, None, :] * sine[None]
    return table.reshape(len(waves), len(positions))


def plain(state, to_modes, from_modes, mode_depth):
    wide, lev = lax.axis_size("wide"), lax.axis_size("lev")
    devices = wide * lev
    levels, rows, cols = state.shape
    length = I + E
    waves = np.arange(-KT, KT)
    share = len(waves) // devices
    table = cas_table(waves, np.arange(length), length)
    spec = jnp.einsum("qn,lrn->qlr", table, extend(state, E), precision=HIGH)
    spec = spec.reshape(devices, share, levels * rows)
    spec = lax.all_to_all(spec, AXES, 0, 0, tiled=True)
    spec = spec.reshape(wide, lev, share, levels, rows).transpose(1, 3, 2, 0, 4)
    spec = extend(spec.reshape(lev * levels, share, wide * rows), E)
    spec = jnp.einsum("lqr,pr->lqp", spec, table, precision=HIGH)
    first = (lax.axis_index("wide") * lev + lax.axis_index("lev")) * share
    lap = (4.0 * np.sin(np.pi * waves / length) ** 2).astype(np.float32)
    square = (waves * waves).astype(np.int32)
    lap_q = lax.dynamic_slice_in_dim(jnp.asarray(lap), first, share)
    square_q = lax.dynamic_slice_in_dim(jnp.asarray(square), first, share)
    keep = (square_q[:, None] + square[None, :] < KT * KT).astype(jnp.float32)
    modes = jnp.einsum("ml,lqp->mqp", to_modes, spec, precision=HIGHEST)
    solved = modes * keep / (1.0 + mode_depth[:, None, None] * (lap_q[:, None] + lap[None, :]))
    mixed = jnp.einsum("lm,mqp->lqp", from_modes, solved, precision=HIGHEST)
    back = jnp.einsum("lqp,pr->lqr", mixed, table[:, :I], precision=HIGH)
    back = back.reshape(lev, levels, share, wide, rows).transpose(3, 0, 2, 1, 4)
    back = lax.all_to_all(back.reshape(devices, share, levels * rows), AXES, 0, 0, tiled=True)
    back = back.reshape(len(waves), levels, rows)
    return jnp.einsum("qlr,qn->lrn", back, table[:, :I], precision=HIGH) / (length * length)


def split(value):
    high = value.astype(jnp.bfloat16)
    return high, (value - high.astype(jnp.float32)).astype(jnp.bfloat16)


def dot(a, b, contract):
    return lax.dot_general(a, b, (contract, ((), ())), preferred_element_type=jnp.float32)


def left_half():
    return lax.broadcasted_iota(jnp.int32, (1, LANES), 1) < HALF


def swap(value):
    return pltpu.roll(value, HALF, 1)


def at(start, size, unit):
    return pl.ds(start if isinstance(start, int) else pl.multiple_of(start, unit), size)


def fill_table(seeds, first, high, low):
    plus, minus, cosine, sine = seeds
    cosines, sines = cosine[...], sine[...]
    for group in range(high.shape[0] // STEP):
        rows = slice(group * STEP, (group + 1) * STEP)
        pick = pl.ds(first + group, 1)
        high[rows], low[rows] = split(plus[pick] * cosines + minus[pick] * sines)


def forward_x(chunk, odd, x, edge, *refs, with_y):
    levels, rows, cols = x.shape
    seeds, refs = refs[:4], refs[4:]
    if with_y:
        seeds_y, refs = refs[:4], refs[4:]
        out, high, low, y_high, y_low, xs_high, xs_low = refs
    else:
        out, high, low, xs_high, xs_low = refs
    step = pl.program_id(0)

    @pl.when(step == 0)
    def _():
        whole = cols // LANES * LANES

        def place(start, value):
            extra = sum(value[:, c : c + 1] * edge[i : i + 1] for i, c in enumerate((0, 1, cols - 2, cols - 1)))
            rest = value[:, whole:]
            last = jnp.concatenate([rest, jnp.zeros_like(rest)], axis=1) + extra
            where = at(start, value.shape[0], HALF)
            xs_high[where, :whole], xs_low[where, :whole] = split(value[:, :whole])
            xs_high[where, whole:], xs_low[where, whole:] = split(last)

        blank = jnp.zeros((LANES + HALF - rows, cols), jnp.float32)
        flag = odd[0]
        for level in range(levels):
            place(level * LANES, x[level, :LANES])
            rest = jnp.concatenate([x[level, LANES:], blank], axis=0)
            if level < 2:
                place(levels * LANES + HALF * (flag if level == 0 else 1 - flag), rest)
            else:
                place((levels + 1) * LANES, rest)
                place((levels + 1) * LANES + HALF, rest)

    fill_table(seeds, chunk + step * (high.shape[0] // STEP), high, low)
    if with_y:
        fill_table(seeds_y, step * (y_high.shape[0] // STEP), y_high, y_low)
    t_high = high[...]
    across = ((1,), (1,))
    spec = dot(t_high, xs_high[...], across) + (dot(low[...], xs_high[...], across) + dot(t_high, xs_low[...], across))
    left = left_half()
    for d in range(out.shape[0]):
        part = spec[d * STEP : (d + 1) * STEP]
        for piece in range(levels + 1):
            out[d, piece * STEP : (piece + 1) * STEP] = part[:, piece * LANES : (piece + 1) * LANES]
        last = part[:, (levels + 1) * LANES :]
        out[d, (levels + 1) * STEP :] = jnp.where(left, last[: STEP // 2], last[STEP // 2 :])


def middle(
    chunk, devices, me, to_modes, from_modes, depth, got, high, low, edge, own, line, out, xs, ms, ends, *, wide, tail
):
    count = got.shape[0]
    lev = count // wide
    total = to_modes.shape[0]
    levels = total // lev
    span = total * STEP
    left = left_half()
    rem = slice(levels * STEP, (levels + 1) * STEP)
    rem2 = slice((levels + 1) * STEP, (levels + 1) * STEP + STEP // 2)

    def rows_of(lv, level):
        start = (lv * levels + level) * STEP
        return start, slice(start, start + STEP)

    for lv in range(lev):
        first_src, last_src = lv, (wide - 1) * lev + lv
        for level in range(levels):
            start, rows = rows_of(lv, level)
            ends[rows, 0:2] = got[first_src, level * STEP : (level + 1) * STEP, 0:2]
            if level < 2:
                lane = (HALF if level == 0 else 0) + tail - 2
                ends[rows, 2:4] = got[last_src, rem, lane : lane + 2]
            else:
                ends[start : start + STEP // 2, 2:4] = got[last_src, rem2, tail - 2 : tail]
                ends[start + STEP // 2 : start + STEP, 2:4] = got[last_src, rem2, HALF + tail - 2 : HALF + tail]

    def gather(pair, carry):
        weights = edge[:, at(pair * LANES, LANES, LANES)]

        def put(start, size, lanes, value):
            for base, part in zip((0, span), split(value)):
                xs[base + start : base + start + size, lanes] = part

        for lv in range(lev):
            even, uneven = 2 * pair * lev + lv, (2 * pair + 1) * lev + lv
            for level in range(levels):
                start, rows = rows_of(lv, level)
                full = slice(level * STEP, (level + 1) * STEP)
                put(start, STEP, at(2 * pair * LANES, LANES, LANES), got[even, full])
                put(start, STEP, at((2 * pair + 1) * LANES, LANES, LANES), got[uneven, full])
                if level < 2:
                    a, b = got[even, rem], got[uneven, rem]
                    value = jnp.where(left, a, b) if level == 0 else swap(jnp.where(left, b, a))
                else:
                    a, b = got[even, rem2], got[uneven, rem2]
                    value = jnp.concatenate([jnp.where(left, a, swap(b)), jnp.where(left, swap(a), b)], axis=0)
                for i in range(4):
                    value = value + ends[rows, i : i + 1] * weights[i : i + 1]
                put(start, STEP, at(wide * LANES + pair * LANES, LANES, LANES), value)
        return carry

    lax.fori_loop(0, wide // 2, gather, 0)

    group = chunk * devices + me[0]
    mine = lax.broadcasted_iota(jnp.int32, (1, LANES), 1) == group
    lap_q = jnp.sum(jnp.where(mine, own[0], 0.0), axis=1, keepdims=True)
    square_q = jnp.sum(jnp.where(mine, own[1], 0.0), axis=1, keepdims=True)
    length = high.shape[1]

    def solve(tile, carry):
        where = at(tile * TILE, TILE, TILE)
        across = ((1,), (1,))
        both = dot(xs[...], high[where], across)
        spec = both[:span] + (both[span:] + dot(xs[:span], low[where], across))
        for half in range(TILE // LANES):
            lanes = slice(half * LANES, (half + 1) * LANES)
            here = at(tile * TILE + half * LANES, LANES, LANES)
            lap = lap_q + line[0:1, here]
            scale = jnp.where(square_q + line[1:2, here] < float(KT * KT), 1.0 / (length * length), 0.0)
            parts = [spec[l * STEP : (l + 1) * STEP, lanes] for l in range(total)]
            solved = []
            for m in range(total):
                mode = sum(to_modes[m, l] * parts[l] for l in range(total))
                solved.append(mode * scale / (1.0 + depth[m] * lap))
            for l in range(total):
                mixed = sum(from_modes[l, m] * solved[m] for m in range(total))
                for base, part in zip((0, span), split(mixed)):
                    ms[base + l * STEP : base + (l + 1) * STEP, here] = part
        return carry

    lax.fori_loop(0, high.shape[0] // TILE, solve, 0)

    def back(start):
        where = at(start, TILE, TILE)
        down = ((1,), (0,))
        both = dot(ms[...], high[:, where], down)
        return both[:span] + (both[span:] + dot(ms[:span], low[:, where], down))

    def scatter(pair, carry):
        value = back(pair * TILE)
        for half in range(2):
            for lv in range(lev):
                for level in range(levels):
                    _, rows = rows_of(lv, level)
                    out[(2 * pair + half) * lev + lv, level * STEP : (level + 1) * STEP] = value[
                        rows, half * LANES : (half + 1) * LANES
                    ]
        return carry

    lax.fori_loop(0, wide // 2, scatter, 0)

    def scatter_rest(quad, carry):
        value = back(wide * LANES + quad * TILE)
        for half in range(2):
            pair = 2 * quad + half
            lanes = slice(half * LANES, (half + 1) * LANES)
            for lv in range(lev):
                even, uneven = 2 * pair * lev + lv, (2 * pair + 1) * lev + lv
                a, b = value[rows_of(lv, 0)[1], lanes], swap(value[rows_of(lv, 1)[1], lanes])
                out[even, rem] = jnp.where(left, a, b)
                out[uneven, rem] = jnp.where(left, b, a)
                start = rows_of(lv, 2)[0]
                a, b = value[start : start + STEP // 2, lanes], value[start + STEP // 2 : start + STEP, lanes]
                out[even, rem2] = jnp.where(left, a, swap(b))
                out[uneven, rem2] = jnp.where(left, swap(a), b)
        return carry

    lax.fori_loop(0, wide // 4, scatter_rest, 0)


def inverse_x(odd, got, high, low, *refs, more):
    prior, refs = (refs[0], refs[1:]) if more else (None, refs)
    out, zs = refs
    levels, rows, _ = out.shape
    span = zs.shape[0] // 2
    waves = zs.shape[1]

    @pl.when(pl.program_id(0) == 0)
    def _():
        def place(start, value):
            size = min(LANES, span - start)
            turned = value.reshape(waves, LANES).T[:size]
            for base, part in zip((0, span), split(turned)):
                zs[base + start : base + start + size] = part

        for piece in range(levels + 1):
            place(piece * LANES, got[:, piece * STEP : (piece + 1) * STEP])
        last = got[:, (levels + 1) * STEP :]
        turned = swap(last.reshape(waves // 2, LANES)).reshape(last.shape)
        place((levels + 1) * LANES, jnp.concatenate([last, turned], axis=1))

    down = ((1,), (0,))
    both = dot(zs[...], high[...], down)
    value = both[:span] + (both[span:] + dot(zs[:span], low[...], down))
    flag = odd[0]
    rest = rows - LANES
    places = [(level, slice(0, LANES), level * LANES) for level in range(levels)]
    for level, start in ((flag, levels * LANES), (1 - flag, levels * LANES + HALF), (2, (levels + 1) * LANES)):
        places.append((level, slice(LANES, rows), start))
    for level, where, start in places:
        part = value[start : start + where.stop - where.start]
        out[level, where] = part + prior[level, where] if more else part


def packs(wide, lev, levels, rows, cols):
    share = 2 * KT // (wide * lev)
    return (
        levels == 3
        and wide % 4 == 0
        and LANES < rows <= LANES + HALF
        and (LANES + HALF - rows) * wide == E
        and cols % LANES == HALF == E
        and (cols + E) % TILE == 0
        and (wide * lev * STEP) % TILE == 0
        and share % STEP == 0
        and 2 * KT // STEP <= LANES
    )


def packed(state, to_modes, from_modes, mode_depth):
    wide, lev = lax.axis_size("wide"), lax.axis_size("lev")
    levels, rows, cols = state.shape
    devices = wide * lev
    length = cols + E
    chunks = 2 * KT // (devices * STEP)
    width = devices * STEP
    tail = rows - LANES
    extra = E // wide
    block = (levels + 1) * STEP + STEP // 2
    total = lev * levels
    f32, bf16 = jnp.float32, jnp.bfloat16

    waves = np.arange(-KT, KT)
    columns = np.arange(length)
    starts = np.arange(wide)[:, None]
    order = np.concatenate(
        [
            (starts * rows + np.arange(LANES)).reshape(-1),
            np.concatenate(
                [starts * rows + LANES + np.arange(tail), cols + starts * extra + np.arange(extra)], axis=1
            ).reshape(-1),
        ]
    )
    seeds_x = [jnp.asarray(a) for a in cas_seeds(waves, columns, length)]
    seeds_y = [jnp.asarray(a) for a in cas_seeds(waves, order, length)]
    weights = edge_weights(E)
    edge_x = np.concatenate([np.zeros((4, HALF), np.float32), weights], axis=1)
    edge_y = np.zeros((4, length), np.float32)
    edge_y[:, order >= cols] = weights[:, order[order >= cols] - cols]
    edge_y = edge_y[:, wide * LANES :]
    lap = (4.0 * np.sin(np.pi * waves / length) ** 2).astype(np.float32)
    line = np.stack([lap, (waves * waves).astype(np.float32)])
    own = np.zeros((2, STEP, LANES), np.float32)
    own[:, :, : len(waves) // STEP] = line.reshape(2, -1, STEP).transpose(0, 2, 1)

    odd = lax.rem(lax.axis_index("wide"), 2).reshape(1)
    me = (lax.axis_index("wide") * lev + lax.axis_index("lev")).reshape(1)
    smem = pl.BlockSpec(memory_space=pltpu.SMEM)
    vmem = pl.BlockSpec(memory_space=pltpu.VMEM)
    params = pltpu.CompilerParams(vmem_limit_bytes=56 << 20)

    def whole(a):
        return pl.BlockSpec(a.shape, lambda i: (0,) * a.ndim)

    def cost(flops, size):
        return pl.CostEstimate(flops=flops, bytes_accessed=size, transcendentals=0)

    def to_columns(chunk):
        with_y = chunk == chunks - 1
        steps = width // TILE
        operands = [state, jnp.asarray(edge_x), *seeds_x] + (seeds_y if with_y else [])
        shapes = [((devices, block, LANES), f32), ((width, length), bf16), ((width, length), bf16)]
        if with_y:
            shapes += [((2 * KT, length), bf16)] * 2
        span = (levels + 2) * LANES
        return pl.pallas_call(
            functools.partial(forward_x, chunk * devices, with_y=with_y),
            grid=(steps,),
            in_specs=[smem] + [whole(a) for a in operands],
            out_specs=[
                pl.BlockSpec((s[0] // steps, *s[1:]), lambda i, n=len(s): (i,) + (0,) * (n - 1)) for s, _ in shapes
            ],
            out_shape=[jax.ShapeDtypeStruct(s, d) for s, d in shapes],
            scratch_shapes=[pltpu.VMEM((span, length), bf16)] * 2,
            compiler_params=params,
            cost_estimate=cost(6 * width * span * length, 8 << 20),
            name=f"forward_x_{chunk}",
        )(odd, *operands)

    def through(chunk, got, high, low):
        operands = [got, high, low, jnp.asarray(edge_y), jnp.asarray(own), jnp.asarray(line)]
        span = total * STEP
        return pl.pallas_call(
            functools.partial(middle, chunk, devices, wide=wide, tail=tail),
            in_specs=[smem] * 4 + [vmem] * len(operands),
            out_specs=vmem,
            out_shape=jax.ShapeDtypeStruct(got.shape, f32),
            scratch_shapes=[
                pltpu.VMEM((2 * span, length), bf16),
                pltpu.VMEM((2 * span, 2 * KT), bf16),
                pltpu.VMEM((span, LANES), f32),
            ],
            compiler_params=params,
            cost_estimate=cost(12 * span * 2 * KT * length, 9 << 20),
            name=f"middle_{chunk}",
        )(me, to_modes, from_modes, mode_depth, *operands)

    def to_rows(got, high, low, prior):
        span = (levels + 1) * LANES + HALF
        tables = pl.BlockSpec((width, TILE), lambda i: (0, i))
        sums = pl.BlockSpec((levels, rows, TILE), lambda i: (0, 0, i))
        more = prior is not None
        return pl.pallas_call(
            functools.partial(inverse_x, more=more),
            grid=(length // TILE,),
            in_specs=[smem, whole(got), tables, tables] + [sums] * more,
            out_specs=sums,
            out_shape=jax.ShapeDtypeStruct(state.shape, f32),
            scratch_shapes=[pltpu.VMEM((2 * span, width), bf16)],
            compiler_params=params,
            cost_estimate=cost(6 * width * span * length, 8 << 20),
            name="inverse_x",
        )(odd, got, high, low, *([prior] if more else []))

    def exchange(sent):
        return lax.all_to_all(sent, AXES, 0, 0, tiled=True)

    tables, arrived = [], []
    for chunk in range(chunks):
        sent, high, low, *table_y = to_columns(chunk)
        tables.append((high, low))
        arrived.append(exchange(sent))
    returned = [exchange(through(chunk, got, *table_y)) for chunk, got in enumerate(arrived)]
    value = None
    for got, table in zip(returned, tables):
        value = to_rows(got, *table, value)
    return value


def solution(mesh):
    placed = (P("lev", "wide", None), P(), P(), P())

    def shards(state, *rest):
        fits = packs(lax.axis_size("wide"), lax.axis_size("lev"), *state.shape)
        return (packed if fits else plain)(state, *rest)

    return jax.shard_map(
        shards, mesh=mesh, in_specs=placed, out_specs=P("lev", "wide", None), check_vma=False
    )
```

```python
import functools

import jax
import jax.numpy as jnp
import numpy as np
from jax import lax
from jax.experimental import pallas as pl
from jax.experimental.pallas import tpu as pltpu
from jax.sharding import PartitionSpec as P

I = 1472
E = 64
KT = 512
STEP = 16
LANES = 128
HALF = 64
TILE = 256

HIGH = lax.Precision.HIGH
HIGHEST = lax.Precision.HIGHEST
AXES = ("wide", "lev")


def blend_weights(extra):
    f = (np.arange(extra, dtype=np.float64) + 1.0) / (extra + 1.0)
    f2, f3 = f * f, f * f * f
    return 2 * f3 - 3 * f2 + 1, f3 - 2 * f2 + f, -2 * f3 + 3 * f2, f3 - f2


def edge_weights(extra):
    h00, h10, h01, h11 = blend_weights(extra)
    return np.stack([h01 - h11, h11, -h10, h00 + h10]).astype(np.float32)


def extend(block, extra):
    w = jnp.asarray(edge_weights(extra))
    added = (
        block[..., :1] * w[0] + block[..., 1:2] * w[1] + block[..., -2:-1] * w[2] + block[..., -1:] * w[3]
    )
    return jnp.concatenate([block, added], axis=-1)


def cas_seeds(waves, positions, length):
    turn = 2.0 * np.pi / length
    base = waves[::STEP].astype(np.int64)
    coarse = turn * ((base[:, None] * positions[None, :]) % length)
    fine = turn * ((np.arange(STEP)[:, None] * positions[None, :]) % length)
    parts = np.cos(coarse) + np.sin(coarse), np.cos(coarse) - np.sin(coarse), np.cos(fine), np.sin(fine)
    return [np.asarray(a, np.float32) for a in parts]


def cas_table(waves, positions, length):
    plus, minus, cosine, sine = (jnp.asarray(a) for a in cas_seeds(waves, positions, length))
    table = plus[:, None, :] * cosine[None] + minus[:, None, :] * sine[None]
    return table.reshape(len(waves), len(positions))


def plain(state, to_modes, from_modes, mode_depth):
    wide, lev = lax.axis_size("wide"), lax.axis_size("lev")
    devices = wide * lev
    levels, rows, cols = state.shape
    length = I + E
    waves = np.arange(-KT, KT)
    share = len(waves) // devices
    table = cas_table(waves, np.arange(length), length)
    spec = jnp.einsum("qn,lrn->qlr", table, extend(state, E), precision=HIGH)
    spec = spec.reshape(devices, share, levels * rows)
    spec = lax.all_to_all(spec, AXES, 0, 0, tiled=True)
    spec = spec.reshape(wide, lev, share, levels, rows).transpose(1, 3, 2, 0, 4)
    spec = extend(spec.reshape(lev * levels, share, wide * rows), E)
    spec = jnp.einsum("lqr,pr->lqp", spec, table, precision=HIGH)
    first = (lax.axis_index("wide") * lev + lax.axis_index("lev")) * share
    lap = (4.0 * np.sin(np.pi * waves / length) ** 2).astype(np.float32)
    square = (waves * waves).astype(np.int32)
    lap_q = lax.dynamic_slice_in_dim(jnp.asarray(lap), first, share)
    square_q = lax.dynamic_slice_in_dim(jnp.asarray(square), first, share)
    keep = (square_q[:, None] + square[None, :] < KT * KT).astype(jnp.float32)
    modes = jnp.einsum("ml,lqp->mqp", to_modes, spec, precision=HIGHEST)
    solved = modes * keep / (1.0 + mode_depth[:, None, None] * (lap_q[:, None] + lap[None, :]))
    mixed = jnp.einsum("lm,mqp->lqp", from_modes, solved, precision=HIGHEST)
    back = jnp.einsum("lqp,pr->lqr", mixed, table[:, :I], precision=HIGH)
    back = back.reshape(lev, levels, share, wide, rows).transpose(3, 0, 2, 1, 4)
    back = lax.all_to_all(back.reshape(devices, share, levels * rows), AXES, 0, 0, tiled=True)
    back = back.reshape(len(waves), levels, rows)
    return jnp.einsum("qlr,qn->lrn", back, table[:, :I], precision=HIGH) / (length * length)


LIMITS = (16, 16, 10, 16)


def split(value):
    high = value.astype(jnp.bfloat16)
    return high, (value - high.astype(jnp.float32)).astype(jnp.bfloat16)


def dot(a, b, contract):
    return lax.dot_general(a, b, (contract, ((), ())), preferred_element_type=jnp.float32)


def left_half():
    return lax.broadcasted_iota(jnp.int32, (1, LANES), 1) < HALF


def swap(value):
    return pltpu.roll(value, HALF, 1)


def mirror(value):
    order = LANES - 1 - lax.broadcasted_iota(jnp.int32, value.shape, 1)
    return jnp.take_along_axis(value, order, axis=1)


def at(start, size, unit):
    return pl.ds(start if isinstance(start, int) else pl.multiple_of(start, unit), size)


def fill_tables(seeds, first, cos_high, cos_low, sin_high, sin_low):
    coarse_cos, coarse_sin, fine_cos, fine_sin = seeds
    for lane in range(0, cos_high.shape[-1], TILE):
        lanes = slice(lane, lane + TILE)
        fine_c, fine_s = fine_cos[:, lanes], fine_sin[:, lanes]
        for group in range(cos_high.shape[0] // STEP):
            rows = slice(group * STEP, (group + 1) * STEP)
            pick = pl.ds(first + group, 1)
            coarse_c, coarse_s = coarse_cos[pick, lanes], coarse_sin[pick, lanes]
            cos_high[rows, lanes], cos_low[rows, lanes] = split(coarse_c * fine_c - coarse_s * fine_s)
            sin_high[rows, lanes], sin_low[rows, lanes] = split(coarse_s * fine_c + coarse_c * fine_s)


def make_tables(order, *refs):
    seeds_x, seeds_y, tables_x, (high, low) = refs[:4], refs[4:8], refs[8:12], refs[12:]
    first = pl.program_id(0) * (tables_x[0].shape[0] // STEP)
    fill_tables(seeds_x, first, *tables_x)
    fill_tables(seeds_y, first, high.at[0], low.at[0], high.at[1], low.at[1])


def forward_x(chunk, place, x, edge, *refs):
    seeds, (out, *tables, even, uneven, buffer, packed, in_sems, out_sems) = refs[:4], refs[4:]
    levels, rows, cols = x.shape
    waves = tables[0].shape[0]
    groups = waves // 8
    size = LANES + HALF
    half = tables[0].shape[1]
    step = pl.program_id(0)
    odd, upper = place[0], place[1]
    rest = rows - LANES
    block = 32

    def fetch(level):
        return pltpu.make_async_copy(x.at[level], buffer.at[level], in_sems.at[level])

    def send(level):
        first = level * STEP
        count = STEP if level < levels - 1 else packed.shape[1] - first
        piece = slice(first, first + count)
        return pltpu.make_async_copy(packed.at[:, piece], out.at[:, piece], out_sems.at[level])

    @pl.when(step == 0)
    def _():
        for level in range(levels):
            fetch(level).start()
        fill_tables(seeds, chunk * (waves // STEP), *tables)

    for level in range(levels):

        @pl.when(step == level)
        def _():
            fetch(level).wait()
            for r in range(0, size, block):

                def read(lanes):
                    if r < LANES:
                        return buffer[level, at(rest * upper + r, block, 8), lanes]
                    first = r - LANES
                    live = min(block, rest - first)
                    low = buffer[level, LANES + first : LANES + first + live, lanes]
                    if live < block:
                        low = jnp.concatenate([low, jnp.zeros((block - live, low.shape[1]), low.dtype)], axis=0)
                    shift = HALF - rest
                    if first < shift:
                        high = buffer[level, 0 : block - shift, lanes]
                        high = jnp.concatenate([jnp.zeros((shift, high.shape[1]), high.dtype), high], axis=0)
                    else:
                        high = buffer[level, first - shift : first - shift + block, lanes]
                    return jnp.where(upper == 1, high, low)

                where = slice(r, r + block)
                above = slice(size + r, size + r + block)
                for tile in range(half // LANES):
                    lanes = slice(tile * LANES, (tile + 1) * LANES)
                    value = read(lanes)
                    start = cols + HALF - (tile + 1) * LANES
                    other = read(slice(start, min(start + LANES, cols)))
                    if tile == 0:
                        ends = (value[:, 0:1], value[:, 1:2], other[:, HALF - 2 : HALF - 1], other[:, HALF - 1 : HALF])
                        other = jnp.concatenate([other, jnp.zeros_like(other)], axis=1)
                        for i, end in enumerate(ends):
                            other = other + end * edge[i : i + 1]
                    other = mirror(other)
                    even[where, lanes], even[above, lanes] = split(value + other)
                    uneven[where, lanes], uneven[above, lanes] = split(value - other)

            across = ((1,), (1,))
            blank = jnp.zeros((HALF, waves), jnp.float32)
            for part, (source, high, low) in enumerate(((even, *tables[:2]), (uneven, *tables[2:]))):
                both = dot(source[...], high[...], across)
                spec = both[:size] + (both[size:] + dot(source[:size], low[...], across))
                full = spec[:LANES].T
                first = level * STEP + part * 8
                packed[:, first : first + 8] = full.reshape(groups, 8, LANES)
                if level < 2:
                    first = levels * STEP + part * 8
                    if level == 0:
                        turned = jnp.concatenate([spec[LANES:], blank], axis=0).T
                        packed[:, first : first + 8] = turned.reshape(groups, 8, LANES)
                    else:
                        turned = jnp.concatenate([blank, spec[LANES:]], axis=0).T
                        value = packed[:, first : first + 8].reshape(waves, LANES) + turned
                        value = jnp.where(odd == 1, swap(value), value)
                        packed[:, first : first + 8] = value.reshape(groups, 8, LANES)
                else:
                    pieces = [spec[LANES:], blank] if part == 0 else [blank, spec[LANES:]]
                    turned = jnp.concatenate(pieces, axis=0).T.reshape(groups, 8, LANES)
                    first = (levels + 1) * STEP
                    if part == 0:
                        packed[:, first : first + 8] = turned
                    else:
                        packed[:, first : first + 8] = packed[:, first : first + 8] + turned
            send(level).start()

    @pl.when(step == levels - 1)
    def _():
        for level in range(levels):
            send(level).wait()


def middle(
    chunk, devices, me, to_modes, from_modes, depth, got, *refs, wide
):
    high, low, edge, own, line, out, xs, ms, ends = refs
    count = got.shape[0]
    lev = count // wide
    total = to_modes.shape[0]
    levels = total // lev
    span = total * STEP
    pairs = wide // 2
    left = left_half()
    rem = slice(levels * STEP, (levels + 1) * STEP)
    rem2 = slice((levels + 1) * STEP, (levels + 1) * STEP + STEP // 2)
    half = high.shape[1]
    waves = high.shape[0] // 2

    def rows_of(lv, level):
        start = (lv * levels + level) * STEP
        return start, slice(start, start + STEP)

    for lv in range(lev):
        for level in range(levels):
            rows = rows_of(lv, level)[1]
            full = slice(level * STEP, (level + 1) * STEP)
            ends[rows, 0:2] = got[lv, full, 0:2]
            ends[rows, 2:4] = got[(wide - 1) * lev + lv, full, LANES - 2 : LANES]

    def put(part, start, lanes, value):
        for base, piece in zip((0, span), split(value)):
            xs[part, base + start : base + start + value.shape[0], lanes] = piece

    def gather(pair, carry):
        weights = edge[:, :, at(pair * LANES, LANES, LANES)]
        for lv in range(lev):
            a, b = 2 * pair, 2 * pair + 1
            low_a, low_b = a * lev + lv, b * lev + lv
            top_a, top_b = (wide - 1 - a) * lev + lv, (wide - 1 - b) * lev + lv
            for level in range(levels):
                start = rows_of(lv, level)[0]
                full = slice(level * STEP, (level + 1) * STEP)
                for w, src, top in ((a, low_a, top_a), (b, low_b, top_b)):
                    value, other = got[src, full], mirror(got[top, full])
                    lanes = at(w * LANES, LANES, LANES)
                    put(0, start, lanes, value + other)
                    put(1, start, lanes, value - other)
            turned = mirror(got[top_a, rem]), mirror(got[top_b, rem])
            turned2 = swap(mirror(got[top_a, rem2])), swap(mirror(got[top_b, rem2]))
            for part, sign in ((0, 1.0), (1, -1.0)):
                fa, fb = got[low_a, rem] + sign * turned[0], got[low_b, rem] + sign * turned[1]
                ga, gb = got[low_a, rem2] + sign * turned2[0], got[low_b, rem2] + sign * turned2[1]
                values = (
                    jnp.where(left, fa, fb),
                    swap(jnp.where(left, fb, fa)),
                    jnp.concatenate([jnp.where(left, ga, swap(gb)), jnp.where(left, swap(ga), gb)], axis=0),
                )
                for level, value in enumerate(values):
                    start, rows = rows_of(lv, level)
                    for i in range(4):
                        value = value + ends[rows, i : i + 1] * weights[part, i : i + 1]
                    put(part, start, at(pairs * LANES + pair * LANES, LANES, LANES), value)
        return carry

    lax.fori_loop(0, pairs // 2, gather, 0)

    group = chunk * devices + me[0]
    mine = lax.broadcasted_iota(jnp.int32, (1, LANES), 1) == group
    lap_q, square_q, weight_q = (
        jnp.sum(jnp.where(mine, own[i], 0.0), axis=1, keepdims=True) for i in range(3)
    )

    def solve(tile, carry):
        where = at(tile * TILE, TILE, TILE)
        part = tile // (waves // TILE)
        across = ((1,), (1,))
        both = dot(xs[part], high[where], across)
        spec = both[:span] + (both[span:] + dot(xs[part, :span], low[where], across))
        for piece in range(TILE // LANES):
            lanes = slice(piece * LANES, (piece + 1) * LANES)
            here = at(tile * TILE + piece * LANES, LANES, LANES)
            lap = lap_q + line[0:1, here]
            scale = jnp.where(square_q + line[1:2, here] < float(KT * KT), weight_q * line[2:3, here], 0.0)
            parts = [spec[l * STEP : (l + 1) * STEP, lanes] for l in range(total)]
            solved = []
            for m in range(total):
                mode = sum(to_modes[m, l] * parts[l] for l in range(total))
                solved.append(mode * scale / (1.0 + depth[m] * lap))
            for l in range(total):
                mixed = sum(from_modes[l, m] * solved[m] for m in range(total))
                for base, value in zip((0, span), split(mixed)):
                    ms[base + l * STEP : base + (l + 1) * STEP, here] = value
        return carry

    lax.fori_loop(0, 2 * waves // TILE, solve, 0)

    def back(start):
        where = at(start, TILE, TILE)
        down = ((1,), (0,))
        sums = []
        for part in range(2):
            k = slice(part * waves, (part + 1) * waves)
            both = dot(ms[:, k], high[k, where], down)
            sums.append(both[:span] + (both[span:] + dot(ms[:span, k], low[k, where], down)))
        return sums[0] + sums[1], sums[0] - sums[1]

    def scatter(pair, carry):
        values = back(pair * TILE)
        for piece in range(2):
            w = 2 * pair + piece
            lanes = slice(piece * LANES, (piece + 1) * LANES)
            for lv in range(lev):
                for level in range(levels):
                    rows = rows_of(lv, level)[1]
                    full = slice(level * STEP, (level + 1) * STEP)
                    out[w * lev + lv, full] = values[0][rows, lanes]
                    out[(wide - 1 - w) * lev + lv, full] = mirror(values[1][rows, lanes])
        return carry

    lax.fori_loop(0, pairs // 2, scatter, 0)

    for quad in range(pairs // 4):
        values = back(pairs * LANES + quad * TILE)
        for piece in range(2):
            pair = 2 * quad + piece
            lanes = slice(piece * LANES, (piece + 1) * LANES)
            for lv in range(lev):
                packs_of = []
                for value in values:
                    zero, one, two = (value[rows_of(lv, level)[1], lanes] for level in range(3))
                    one = swap(one)
                    cos, sin = two[: STEP // 2], two[STEP // 2 :]
                    packs_of.append(
                        (
                            (jnp.where(left, zero, one), jnp.where(left, cos, swap(sin))),
                            (jnp.where(left, one, zero), jnp.where(left, swap(cos), sin)),
                        )
                    )
                for i in range(2):
                    w = 2 * pair + i
                    out[w * lev + lv, rem], out[w * lev + lv, rem2] = packs_of[0][i]
                    top = (wide - 1 - w) * lev + lv
                    out[top, rem], out[top, rem2] = mirror(packs_of[1][i][0]), swap(mirror(packs_of[1][i][1]))


def inverse_x(chunk, place, got, *refs, more):
    sources, refs = refs[:4], refs[4:]
    prior, refs = (refs[0], refs[1:]) if more else (None, refs)
    out, zs, rems, *tables, sems = refs
    _, rows, cols = out.shape
    waves, half = tables[0].shape
    levels = 3
    size = LANES + HALF
    step = pl.program_id(0)
    odd, upper = place[0], place[1]
    rest = rows - LANES
    fetches = [
        pltpu.make_async_copy(source.at[pl.ds(chunk * waves, waves)], target, sems.at[i])
        for i, (source, target) in enumerate(zip(sources, tables))
    ]

    def turn(start, part):
        return got[:, pl.ds(start + part * 8, 8)].reshape(waves, LANES).T

    @pl.when(step == 0)
    def _():
        for fetch in fetches:
            fetch.start()
        for part in range(2):
            value = turn(levels * STEP, part)
            for i in range(2):
                rems[part, i] = value[i * HALF : (i + 1) * HALF]
        last = got[:, (levels + 1) * STEP :].reshape(waves, LANES).T
        for part in range(2):
            rems[part, 2] = last[part * HALF : (part + 1) * HALF]

    which = jnp.where(step == 2, 2, jnp.where(step == 0, odd, 1 - odd))
    for part in range(2):
        value = turn(pl.multiple_of(step * STEP, STEP), part)
        for base, piece in zip((0, size), split(value)):
            zs[part, base : base + LANES] = piece
        for base, piece in zip((0, size), split(rems[part, which])):
            zs[part, base + LANES : base + size] = piece

    @pl.when(step == 0)
    def _():
        for fetch in fetches:
            fetch.wait()

    down = ((1,), (0,))
    shift = HALF - rest

    def store(lanes, value):
        extra = value.shape[1]
        full, tail = value[:LANES], value[LANES:]
        tail = jnp.where(upper == 1, tail[shift:], tail[:rest])
        for start, piece in ((rest * upper, full), (LANES * (1 - upper), tail)):
            where = at(start, piece.shape[0], 8)
            out[0, where, lanes] = piece + prior[0, where, lanes] if more else piece

    for tile in range(half // TILE):
        where = slice(tile * TILE, (tile + 1) * TILE)
        sums = []
        for part in range(2):
            high, low = tables[2 * part], tables[2 * part + 1]
            both = dot(zs[part], high[:, where], down)
            sums.append(both[:size] + (both[size:] + dot(zs[part, :size], low[:, where], down)))
        store(where, sums[0] + sums[1])
        other = sums[0] - sums[1]
        for piece in range(TILE // LANES):
            start = 2 * half - tile * TILE - (piece + 1) * LANES
            end = min(start + LANES, cols)
            store(slice(start, end), mirror(other[:, piece * LANES : (piece + 1) * LANES])[:, : end - start])


def packs(wide, lev, levels, rows, cols):
    share = 2 * KT // (wide * lev)
    return (
        levels == 3
        and wide % 8 == 0
        and LANES < rows <= LANES + HALF
        and rows % 8 == 0
        and (LANES + HALF - rows) * wide == E
        and cols % LANES == HALF == E
        and (cols + E) % (2 * TILE) == 0
        and (wide * lev * 8) % TILE == 0
        and share % STEP == 0
        and KT // 8 <= LANES
    )


def wave_seeds(doubled, length):
    turn = np.pi / length
    seeds = []
    for waves in (np.arange(0, KT, STEP), np.arange(STEP)):
        angle = turn * ((waves[:, None] * doubled[None, :]) % (2 * length))
        seeds += [np.cos(angle), np.sin(angle)]
    return [np.asarray(a, np.float32) for a in seeds]


def packed(state, to_modes, from_modes, mode_depth):
    wide, lev = lax.axis_size("wide"), lax.axis_size("lev")
    levels, rows, cols = state.shape
    devices = wide * lev
    length = cols + E
    half = length // 2
    chunks = 2 * KT // (devices * STEP)
    width = devices * 8
    tail = rows - LANES
    extra = E // wide
    block = (levels + 1) * STEP + STEP // 2
    total = lev * levels
    f32, bf16 = jnp.float32, jnp.bfloat16

    starts = np.arange(wide // 2)[:, None]
    order = np.concatenate(
        [
            (starts * rows + np.arange(LANES)).reshape(-1),
            np.concatenate(
                [starts * rows + LANES + np.arange(tail), cols + starts * extra + np.arange(extra)], axis=1
            ).reshape(-1),
        ]
    )
    seeds_x = wave_seeds(2 * np.arange(half) + 1, length)
    seeds_y = wave_seeds(2 * order - (cols - 1), length)
    weights = edge_weights(E)
    edge_x = np.concatenate([np.zeros((4, HALF), np.float32), weights], axis=1)
    edge_y = np.zeros((2, 4, half), np.float32)
    outside = order >= cols
    ahead, behind = weights[:, order[outside] - cols], weights[:, E - 1 - (order[outside] - cols)]
    edge_y[0][:, outside], edge_y[1][:, outside] = ahead + behind, ahead - behind
    edge_y = edge_y[:, :, wide // 2 * LANES :]
    waves = np.arange(KT)
    lap = 4.0 * np.sin(np.pi * waves / length) ** 2
    facts = np.stack([lap, waves * waves, np.where(waves == 0, 1.0, 2.0)]).astype(np.float32)
    own = np.zeros((3, STEP, LANES), np.float32)
    own[:, :, : KT // 8] = np.tile(facts.reshape(3, -1, 8).transpose(0, 2, 1), (1, 2, 1))
    line = np.tile(facts, (1, 2))
    line[2] /= length * length

    wide_index = lax.axis_index("wide")
    place = jnp.stack([lax.rem(wide_index, 2), (wide_index >= wide // 2).astype(jnp.int32)])
    me = (wide_index * lev + lax.axis_index("lev")).reshape(1)
    smem = pl.BlockSpec(memory_space=pltpu.SMEM)
    vmem = pl.BlockSpec(memory_space=pltpu.VMEM)
    anywhere = pl.BlockSpec(memory_space=pl.ANY)
    table = (KT, half)

    def params(mib):
        return pltpu.CompilerParams(vmem_limit_bytes=mib << 20)

    def whole(a):
        return pl.BlockSpec(a.shape, lambda i: (0,) * a.ndim)

    def cost(flops, size):
        return pl.CostEstimate(flops=flops, bytes_accessed=size, transcendentals=0)

    def hbm(a):
        return pltpu.with_memory_space_constraint(a, pltpu.HBM)

    def to_columns(chunk):
        operands = [hbm(jnp.asarray(a)) for a in (edge_x, *seeds_x)]
        size = LANES + HALF
        return pl.pallas_call(
            functools.partial(forward_x, chunk),
            grid=(levels,),
            in_specs=[smem, anywhere] + [whole(a) for a in operands],
            out_specs=anywhere,
            out_shape=jax.ShapeDtypeStruct((devices, block, LANES), f32),
            scratch_shapes=[
                *[pltpu.VMEM((width, half), bf16)] * 4,
                *[pltpu.VMEM((2 * size, half), bf16)] * 2,
                pltpu.VMEM(state.shape, f32),
                pltpu.VMEM((devices, block, LANES), f32),
                pltpu.SemaphoreType.DMA((levels,)),
                pltpu.SemaphoreType.DMA((levels,)),
            ],
            compiler_params=params(LIMITS[0]),
            cost_estimate=cost(12 * width * levels * size * half, 8 << 20),
            name=f"forward_x_{chunk}",
        )(place, hbm(state), *operands)

    def all_tables(after):
        operands = [hbm(jnp.asarray(a)) for a in (*seeds_x, *seeds_y)]
        steps = KT // TILE
        return pl.pallas_call(
            make_tables,
            grid=(steps,),
            in_specs=[anywhere] + [whole(a) for a in operands],
            out_specs=[pl.BlockSpec((TILE, half), lambda i: (i, 0))] * 4
            + [pl.BlockSpec((2, TILE, half), lambda i: (0, i, 0))] * 2,
            out_shape=[pltpu.HBM(table, bf16)] * 4 + [jax.ShapeDtypeStruct((2, *table), bf16)] * 2,
            compiler_params=params(LIMITS[1]),
            cost_estimate=cost(32 * KT * half, 8 << 20),
            name="make_tables",
        )(after, *operands)

    def through(chunk, got, high, low):
        operands = [got, high, low, *(jnp.asarray(a) for a in (edge_y, own, line))]
        span = total * STEP
        return pl.pallas_call(
            functools.partial(middle, chunk, devices, wide=wide),
            in_specs=[smem] * 4 + [vmem] * len(operands),
            out_specs=vmem,
            out_shape=jax.ShapeDtypeStruct(got.shape, f32),
            scratch_shapes=[
                pltpu.VMEM((2, 2 * span, half), bf16),
                pltpu.VMEM((2 * span, 2 * KT), bf16),
                pltpu.VMEM((span, LANES), f32),
            ],
            compiler_params=params(LIMITS[2]),
            cost_estimate=cost(24 * span * KT * half, 6 << 20),
            name=f"middle_{chunk}",
        )(me, to_modes, from_modes, mode_depth, *operands)

    def to_rows(chunk, got, tables, prior):
        size = LANES + HALF
        sums = pl.BlockSpec((1, rows, cols), lambda i: (i, 0, 0))
        more = prior is not None
        return pl.pallas_call(
            functools.partial(inverse_x, chunk, more=more),
            grid=(levels,),
            in_specs=[smem, whole(got)] + [anywhere] * 4 + [sums] * more,
            out_specs=sums,
            out_shape=jax.ShapeDtypeStruct(state.shape, f32),
            scratch_shapes=[
                pltpu.VMEM((2, 2 * size, width), bf16),
                pltpu.VMEM((2, levels, HALF, width), f32),
                *[pltpu.VMEM((width, half), bf16)] * 4,
                pltpu.SemaphoreType.DMA((4,)),
            ],
            compiler_params=params(LIMITS[3]),
            cost_estimate=cost(12 * width * levels * size * half, 8 << 20),
            name=f"inverse_x_{chunk}",
        )(place, got, *map(hbm, tables), *([prior] if more else []))

    def exchange(sent):
        return lax.all_to_all(sent, AXES, 0, 0, tiled=True)

    sent = [to_columns(chunk) for chunk in range(chunks)]
    tables = all_tables(sent[-1])
    high, low = (a.reshape(2 * KT, half) for a in tables[4:])
    arrived = [exchange(part) for part in sent]
    returned = [exchange(through(chunk, got, high, low)) for chunk, got in enumerate(arrived)]
    value = None
    for chunk, got in enumerate(returned):
        value = to_rows(chunk, got, tables[:4], value)
    return value


def solution(mesh):
    placed = (P("lev", "wide", None), P(), P(), P())

    def shards(state, *rest):
        fits = packs(lax.axis_size("wide"), lax.axis_size("lev"), *state.shape)
        return (packed if fits else plain)(state, *rest)

    return jax.shard_map(
        shards, mesh=mesh, in_specs=placed, out_specs=P("lev", "wide", None), check_vma=False
    )
```

```python
import functools

import jax
import jax.numpy as jnp
import numpy as np
from jax import lax
from jax.experimental import pallas as pl
from jax.experimental.pallas import tpu as pltpu
from jax.sharding import PartitionSpec as P

I = 1472
E = 64
KT = 512
STEP = 16
LANES = 128
HALF = 64
TILE = 256

HIGH = lax.Precision.HIGH
HIGHEST = lax.Precision.HIGHEST
AXES = ("wide", "lev")


def blend_weights(extra):
    f = (np.arange(extra, dtype=np.float64) + 1.0) / (extra + 1.0)
    f2, f3 = f * f, f * f * f
    return 2 * f3 - 3 * f2 + 1, f3 - 2 * f2 + f, -2 * f3 + 3 * f2, f3 - f2


def edge_weights(extra):
    h00, h10, h01, h11 = blend_weights(extra)
    return np.stack([h01 - h11, h11, -h10, h00 + h10]).astype(np.float32)


def extend(block, extra):
    w = jnp.asarray(edge_weights(extra))
    added = (
        block[..., :1] * w[0] + block[..., 1:2] * w[1] + block[..., -2:-1] * w[2] + block[..., -1:] * w[3]
    )
    return jnp.concatenate([block, added], axis=-1)


def cas_seeds(waves, positions, length):
    turn = 2.0 * np.pi / length
    base = waves[::STEP].astype(np.int64)
    coarse = turn * ((base[:, None] * positions[None, :]) % length)
    fine = turn * ((np.arange(STEP)[:, None] * positions[None, :]) % length)
    parts = np.cos(coarse) + np.sin(coarse), np.cos(coarse) - np.sin(coarse), np.cos(fine), np.sin(fine)
    return [np.asarray(a, np.float32) for a in parts]


def cas_table(waves, positions, length):
    plus, minus, cosine, sine = (jnp.asarray(a) for a in cas_seeds(waves, positions, length))
    table = plus[:, None, :] * cosine[None] + minus[:, None, :] * sine[None]
    return table.reshape(len(waves), len(positions))


def plain(state, to_modes, from_modes, mode_depth):
    wide, lev = lax.axis_size("wide"), lax.axis_size("lev")
    devices = wide * lev
    levels, rows, cols = state.shape
    length = I + E
    waves = np.arange(-KT, KT)
    share = len(waves) // devices
    table = cas_table(waves, np.arange(length), length)
    spec = jnp.einsum("qn,lrn->qlr", table, extend(state, E), precision=HIGH)
    spec = spec.reshape(devices, share, levels * rows)
    spec = lax.all_to_all(spec, AXES, 0, 0, tiled=True)
    spec = spec.reshape(wide, lev, share, levels, rows).transpose(1, 3, 2, 0, 4)
    spec = extend(spec.reshape(lev * levels, share, wide * rows), E)
    spec = jnp.einsum("lqr,pr->lqp", spec, table, precision=HIGH)
    first = (lax.axis_index("wide") * lev + lax.axis_index("lev")) * share
    lap = (4.0 * np.sin(np.pi * waves / length) ** 2).astype(np.float32)
    square = (waves * waves).astype(np.int32)
    lap_q = lax.dynamic_slice_in_dim(jnp.asarray(lap), first, share)
    square_q = lax.dynamic_slice_in_dim(jnp.asarray(square), first, share)
    keep = (square_q[:, None] + square[None, :] < KT * KT).astype(jnp.float32)
    modes = jnp.einsum("ml,lqp->mqp", to_modes, spec, precision=HIGHEST)
    solved = modes * keep / (1.0 + mode_depth[:, None, None] * (lap_q[:, None] + lap[None, :]))
    mixed = jnp.einsum("lm,mqp->lqp", from_modes, solved, precision=HIGHEST)
    back = jnp.einsum("lqp,pr->lqr", mixed, table[:, :I], precision=HIGH)
    back = back.reshape(lev, levels, share, wide, rows).transpose(3, 0, 2, 1, 4)
    back = lax.all_to_all(back.reshape(devices, share, levels * rows), AXES, 0, 0, tiled=True)
    back = back.reshape(len(waves), levels, rows)
    return jnp.einsum("qlr,qn->lrn", back, table[:, :I], precision=HIGH) / (length * length)


LIMITS = (16, 16, 20, 16)


def split(value):
    high = value.astype(jnp.bfloat16)
    return high, (value - high.astype(jnp.float32)).astype(jnp.bfloat16)


def dot(a, b, contract):
    return lax.dot_general(a, b, (contract, ((), ())), preferred_element_type=jnp.float32)


def left_half():
    return lax.broadcasted_iota(jnp.int32, (1, LANES), 1) < HALF


def swap(value):
    return pltpu.roll(value, HALF, 1)


def mirror(value):
    order = LANES - 1 - lax.broadcasted_iota(jnp.int32, value.shape, 1)
    return jnp.take_along_axis(value, order, axis=1)


def empty_lanes(upper, rest):
    lane = lax.broadcasted_iota(jnp.int32, (1, LANES), 1) + rest * upper
    return lax.rem(lane, HALF) >= rest


def dense_rows(rest):
    lasting = STEP + STEP // 2
    return lasting - lasting * (HALF - rest) // HALF, HALF - rest


def fold_rows(read, write, empty, rest):
    kept, gap = dense_rows(rest)
    each = rest // gap
    for j in range(kept):
        moved = pltpu.roll(read(kept + j // each), rest - gap * (j % each), 1)
        write(j, jnp.where(empty, moved, read(j)))


def unfold_rows(read, write, empty, rest):
    kept, gap = dense_rows(rest)
    each = rest // gap
    for i in range(kept // each):
        back = 0.0
        for j in range(i * each, (i + 1) * each):
            value = read(j)
            write(j, jnp.where(empty, 0.0, value))
            back = back + pltpu.roll(jnp.where(empty, value, 0.0), LANES - rest + gap * (j % each), 1)
        write(kept + i, back)


def at(start, size, unit):
    return pl.ds(start if isinstance(start, int) else pl.multiple_of(start, unit), size)


def fill_tables(seeds, first, cos_high, cos_low, sin_high, sin_low):
    coarse_cos, coarse_sin, fine_cos, fine_sin = seeds
    for lane in range(0, cos_high.shape[-1], TILE):
        lanes = slice(lane, lane + TILE)
        fine_c, fine_s = fine_cos[:, lanes], fine_sin[:, lanes]
        for group in range(cos_high.shape[0] // STEP):
            rows = slice(group * STEP, (group + 1) * STEP)
            pick = pl.ds(first + group, 1)
            coarse_c, coarse_s = coarse_cos[pick, lanes], coarse_sin[pick, lanes]
            cos_high[rows, lanes], cos_low[rows, lanes] = split(coarse_c * fine_c - coarse_s * fine_s)
            sin_high[rows, lanes], sin_low[rows, lanes] = split(coarse_s * fine_c + coarse_c * fine_s)


def make_tables(order, *refs):
    seeds_x, seeds_y, tables_x, (high, low) = refs[:4], refs[4:8], refs[8:12], refs[12:]
    first = pl.program_id(0) * (tables_x[0].shape[0] // STEP)
    fill_tables(seeds_x, first, *tables_x)
    fill_tables(seeds_y, first, high.at[0], low.at[0], high.at[1], low.at[1])


def forward_x(chunk, place, x, edge, *refs):
    seeds, (out, *tables, even, uneven, buffer, packed, in_sems) = refs[:4], refs[4:]
    levels, rows, cols = x.shape
    waves = tables[0].shape[0]
    groups = waves // 8
    size = LANES + HALF
    half = tables[0].shape[1]
    step = pl.program_id(0)
    odd, upper = place[0], place[1]
    rest = rows - LANES
    block = 32

    def fetch(level):
        return pltpu.make_async_copy(x.at[level], buffer.at[level], in_sems.at[level])

    height = out.shape[0] // groups

    @pl.when(step == 0)
    def _():
        for level in range(levels):
            fetch(level).start()
        fill_tables(seeds, chunk * (waves // STEP), *tables)

    for level in range(levels):

        @pl.when(step == level)
        def _():
            fetch(level).wait()
            for r in range(0, size, block):

                def read(lanes):
                    if r < LANES:
                        return buffer[level, at(rest * upper + r, block, 8), lanes]
                    first = r - LANES
                    live = min(block, rest - first)
                    low = buffer[level, LANES + first : LANES + first + live, lanes]
                    if live < block:
                        low = jnp.concatenate([low, jnp.zeros((block - live, low.shape[1]), low.dtype)], axis=0)
                    shift = HALF - rest
                    if first < shift:
                        high = buffer[level, 0 : block - shift, lanes]
                        high = jnp.concatenate([jnp.zeros((shift, high.shape[1]), high.dtype), high], axis=0)
                    else:
                        high = buffer[level, first - shift : first - shift + block, lanes]
                    return jnp.where(upper == 1, high, low)

                where = slice(r, r + block)
                above = slice(size + r, size + r + block)
                for tile in range(half // LANES):
                    lanes = slice(tile * LANES, (tile + 1) * LANES)
                    value = read(lanes)
                    start = cols + HALF - (tile + 1) * LANES
                    other = read(slice(start, min(start + LANES, cols)))
                    if tile == 0:
                        ends = (value[:, 0:1], value[:, 1:2], other[:, HALF - 2 : HALF - 1], other[:, HALF - 1 : HALF])
                        other = jnp.concatenate([other, jnp.zeros_like(other)], axis=1)
                        for i, end in enumerate(ends):
                            other = other + end * edge[i : i + 1]
                    other = mirror(other)
                    even[where, lanes], even[above, lanes] = split(value + other)
                    uneven[where, lanes], uneven[above, lanes] = split(value - other)

            across = ((1,), (1,))
            blank = jnp.zeros((HALF, waves), jnp.float32)
            for part, (source, high, low) in enumerate(((even, *tables[:2]), (uneven, *tables[2:]))):
                both = dot(source[...], high[...], across)
                spec = both[:size] + (both[size:] + dot(source[:size], low[...], across))
                full = spec[:LANES].T
                first = level * STEP + part * 8
                for d in range(groups):
                    out[d * height + first : d * height + first + 8] = full[d * 8 : d * 8 + 8]
                if level < 2:
                    first = part * 8
                    if level == 0:
                        turned = jnp.concatenate([spec[LANES:], blank], axis=0).T
                        packed[:, first : first + 8] = turned.reshape(groups, 8, LANES)
                    else:
                        turned = jnp.concatenate([blank, spec[LANES:]], axis=0).T
                        value = packed[:, first : first + 8].reshape(waves, LANES) + turned
                        value = jnp.where(odd == 1, swap(value), value)
                        packed[:, first : first + 8] = value.reshape(groups, 8, LANES)
                else:
                    pieces = [spec[LANES:], blank] if part == 0 else [blank, spec[LANES:]]
                    turned = jnp.concatenate(pieces, axis=0).T.reshape(groups, 8, LANES)
                    first = STEP
                    if part == 0:
                        packed[:, first : first + 8] = turned
                    else:
                        packed[:, first : first + 8] = packed[:, first : first + 8] + turned

    @pl.when(step == levels - 1)
    def _():
        def write(j, value):
            out[pl.ds(levels * STEP + j, groups, stride=height)] = value

        fold_rows(lambda j: packed[:, j], write, empty_lanes(upper, rest), rest)


def middle(
    chunk, devices, me, to_modes, from_modes, depth, arrived, *refs, wide, tail
):
    high, low, edge, own, line, leaving, xs, ms, ends, got, out = refs
    count = got.shape[0]
    lev = count // wide
    total = to_modes.shape[0]
    levels = total // lev
    span = total * STEP
    pairs = wide // 2
    left = left_half()
    rem = slice(levels * STEP, (levels + 1) * STEP)
    rem2 = slice((levels + 1) * STEP, (levels + 1) * STEP + STEP // 2)
    half = high.shape[1]
    waves = high.shape[0] // 2

    def rows_of(lv, level):
        start = (lv * levels + level) * STEP
        return start, slice(start, start + STEP)

    height = arrived.shape[0] // count
    block_index = lax.broadcasted_iota(jnp.int32, (count, 1), 0)
    empty = empty_lanes((block_index >= count // 2).astype(jnp.int32), tail)
    fulls = levels * STEP
    for d in range(count):
        got[d, :fulls] = arrived[d * height : d * height + fulls]

    def keep_row(j, value):
        got[:, fulls + j] = value

    def send_row(j, value):
        leaving[pl.ds(fulls + j, count, stride=height)] = value

    unfold_rows(lambda j: arrived[pl.ds(fulls + j, count, stride=height)], keep_row, empty, tail)

    for lv in range(lev):
        for level in range(levels):
            rows = rows_of(lv, level)[1]
            full = slice(level * STEP, (level + 1) * STEP)
            ends[rows, 0:2] = got[lv, full, 0:2]
            ends[rows, 2:4] = got[(wide - 1) * lev + lv, full, LANES - 2 : LANES]

    def put(part, start, lanes, value):
        for base, piece in zip((0, span), split(value)):
            xs[part, base + start : base + start + value.shape[0], lanes] = piece

    def gather(pair, carry):
        weights = edge[:, :, at(pair * LANES, LANES, LANES)]
        for lv in range(lev):
            a, b = 2 * pair, 2 * pair + 1
            low_a, low_b = a * lev + lv, b * lev + lv
            top_a, top_b = (wide - 1 - a) * lev + lv, (wide - 1 - b) * lev + lv
            for level in range(levels):
                start = rows_of(lv, level)[0]
                full = slice(level * STEP, (level + 1) * STEP)
                for w, src, top in ((a, low_a, top_a), (b, low_b, top_b)):
                    value, other = got[src, full], mirror(got[top, full])
                    lanes = at(w * LANES, LANES, LANES)
                    put(0, start, lanes, value + other)
                    put(1, start, lanes, value - other)
            turned = mirror(got[top_a, rem]), mirror(got[top_b, rem])
            turned2 = swap(mirror(got[top_a, rem2])), swap(mirror(got[top_b, rem2]))
            for part, sign in ((0, 1.0), (1, -1.0)):
                fa, fb = got[low_a, rem] + sign * turned[0], got[low_b, rem] + sign * turned[1]
                ga, gb = got[low_a, rem2] + sign * turned2[0], got[low_b, rem2] + sign * turned2[1]
                values = (
                    jnp.where(left, fa, fb),
                    swap(jnp.where(left, fb, fa)),
                    jnp.concatenate([jnp.where(left, ga, swap(gb)), jnp.where(left, swap(ga), gb)], axis=0),
                )
                for level, value in enumerate(values):
                    start, rows = rows_of(lv, level)
                    for i in range(4):
                        value = value + ends[rows, i : i + 1] * weights[part, i : i + 1]
                    put(part, start, at(pairs * LANES + pair * LANES, LANES, LANES), value)
        return carry

    lax.fori_loop(0, pairs // 2, gather, 0)

    group = chunk * devices + me[0]
    mine = lax.broadcasted_iota(jnp.int32, (1, LANES), 1) == group
    lap_q, square_q, weight_q = (
        jnp.sum(jnp.where(mine, own[i], 0.0), axis=1, keepdims=True) for i in range(3)
    )

    def solve(tile, carry):
        where = at(tile * TILE, TILE, TILE)
        part = tile // (waves // TILE)
        across = ((1,), (1,))
        both = dot(xs[part], high[where], across)
        spec = both[:span] + (both[span:] + dot(xs[part, :span], low[where], across))
        for piece in range(TILE // LANES):
            lanes = slice(piece * LANES, (piece + 1) * LANES)
            here = at(tile * TILE + piece * LANES, LANES, LANES)
            lap = lap_q + line[0:1, here]
            scale = jnp.where(square_q + line[1:2, here] < float(KT * KT), weight_q * line[2:3, here], 0.0)
            parts = [spec[l * STEP : (l + 1) * STEP, lanes] for l in range(total)]
            solved = []
            for m in range(total):
                mode = sum(to_modes[m, l] * parts[l] for l in range(total))
                solved.append(mode * scale / (1.0 + depth[m] * lap))
            for l in range(total):
                mixed = sum(from_modes[l, m] * solved[m] for m in range(total))
                for base, value in zip((0, span), split(mixed)):
                    ms[base + l * STEP : base + (l + 1) * STEP, here] = value
        return carry

    lax.fori_loop(0, 2 * waves // TILE, solve, 0)

    def back(start):
        where = at(start, TILE, TILE)
        down = ((1,), (0,))
        sums = []
        for part in range(2):
            k = slice(part * waves, (part + 1) * waves)
            both = dot(ms[:, k], high[k, where], down)
            sums.append(both[:span] + (both[span:] + dot(ms[:span, k], low[k, where], down)))
        return sums[0] + sums[1], sums[0] - sums[1]

    def scatter(pair, carry):
        values = back(pair * TILE)
        for piece in range(2):
            w = 2 * pair + piece
            lanes = slice(piece * LANES, (piece + 1) * LANES)
            for lv in range(lev):
                for level in range(levels):
                    rows = rows_of(lv, level)[1]
                    full = slice(level * STEP, (level + 1) * STEP)
                    out[w * lev + lv, full] = values[0][rows, lanes]
                    out[(wide - 1 - w) * lev + lv, full] = mirror(values[1][rows, lanes])
        return carry

    lax.fori_loop(0, pairs // 2, scatter, 0)

    for quad in range(pairs // 4):
        values = back(pairs * LANES + quad * TILE)
        for piece in range(2):
            pair = 2 * quad + piece
            lanes = slice(piece * LANES, (piece + 1) * LANES)
            for lv in range(lev):
                packs_of = []
                for value in values:
                    zero, one, two = (value[rows_of(lv, level)[1], lanes] for level in range(3))
                    one = swap(one)
                    cos, sin = two[: STEP // 2], two[STEP // 2 :]
                    packs_of.append(
                        (
                            (jnp.where(left, zero, one), jnp.where(left, cos, swap(sin))),
                            (jnp.where(left, one, zero), jnp.where(left, swap(cos), sin)),
                        )
                    )
                for i in range(2):
                    w = 2 * pair + i
                    out[w * lev + lv, rem], out[w * lev + lv, rem2] = packs_of[0][i]
                    top = (wide - 1 - w) * lev + lv
                    out[top, rem], out[top, rem2] = mirror(packs_of[1][i][0]), swap(mirror(packs_of[1][i][1]))

    for d in range(count):
        leaving[d * height : d * height + fulls] = out[d, :fulls]
    fold_rows(lambda j: out[:, fulls + j], send_row, empty, tail)


def inverse_x(chunk, place, got, *refs, more):
    sources, refs = refs[:4], refs[4:]
    prior, refs = (refs[0], refs[1:]) if more else (None, refs)
    out, zs, rems, *tables, unpacked, sems = refs
    _, rows, cols = out.shape
    waves, half = tables[0].shape
    levels = 3
    size = LANES + HALF
    step = pl.program_id(0)
    odd, upper = place[0], place[1]
    rest = rows - LANES
    fetches = [
        pltpu.make_async_copy(source.at[pl.ds(chunk * waves, waves)], target, sems.at[i])
        for i, (source, target) in enumerate(zip(sources, tables))
    ]

    groups = waves // 8
    height = got.shape[0] // groups

    def turn(start, part):
        first = start + part * 8
        return jnp.concatenate([got[pl.ds(first + d * height, 8)] for d in range(groups)], axis=0).T

    @pl.when(step == 0)
    def _():
        for fetch in fetches:
            fetch.start()

        def keep_row(j, value):
            unpacked[:, j] = value

        unfold_rows(
            lambda j: got[pl.ds(levels * STEP + j, groups, stride=height)], keep_row, empty_lanes(upper, rest), rest
        )
        for part in range(2):
            value = unpacked[:, part * 8 : part * 8 + 8].reshape(waves, LANES).T
            for i in range(2):
                rems[part, i] = value[i * HALF : (i + 1) * HALF]
        last = unpacked[:, STEP:].reshape(waves, LANES).T
        for part in range(2):
            rems[part, 2] = last[part * HALF : (part + 1) * HALF]

    which = jnp.where(step == 2, 2, jnp.where(step == 0, odd, 1 - odd))
    for part in range(2):
        value = turn(pl.multiple_of(step * STEP, STEP), part)
        for base, piece in zip((0, size), split(value)):
            zs[part, base : base + LANES] = piece
        for base, piece in zip((0, size), split(rems[part, which])):
            zs[part, base + LANES : base + size] = piece

    @pl.when(step == 0)
    def _():
        for fetch in fetches:
            fetch.wait()

    down = ((1,), (0,))
    shift = HALF - rest

    def store(lanes, value):
        extra = value.shape[1]
        full, tail = value[:LANES], value[LANES:]
        tail = jnp.where(upper == 1, tail[shift:], tail[:rest])
        for start, piece in ((rest * upper, full), (LANES * (1 - upper), tail)):
            where = at(start, piece.shape[0], 8)
            out[0, where, lanes] = piece + prior[0, where, lanes] if more else piece

    for tile in range(half // TILE):
        where = slice(tile * TILE, (tile + 1) * TILE)
        sums = []
        for part in range(2):
            high, low = tables[2 * part], tables[2 * part + 1]
            both = dot(zs[part], high[:, where], down)
            sums.append(both[:size] + (both[size:] + dot(zs[part, :size], low[:, where], down)))
        store(where, sums[0] + sums[1])
        other = sums[0] - sums[1]
        for piece in range(TILE // LANES):
            start = 2 * half - tile * TILE - (piece + 1) * LANES
            end = min(start + LANES, cols)
            store(slice(start, end), mirror(other[:, piece * LANES : (piece + 1) * LANES])[:, : end - start])


def packs(wide, lev, levels, rows, cols):
    share = 2 * KT // (wide * lev)
    return (
        levels == 3
        and wide % 8 == 0
        and LANES < rows <= LANES + HALF
        and rows % 8 == 0
        and (LANES + HALF - rows) * wide == E
        and cols % LANES == HALF == E
        and (cols + E) % (2 * TILE) == 0
        and (wide * lev * 8) % TILE == 0
        and share % STEP == 0
        and (STEP + STEP // 2) * (LANES + HALF - rows) % HALF == 0
        and (rows - LANES) % (LANES + HALF - rows) == 0
        and KT // 8 <= LANES
    )


def wave_seeds(doubled, length):
    turn = np.pi / length
    seeds = []
    for waves in (np.arange(0, KT, STEP), np.arange(STEP)):
        angle = turn * ((waves[:, None] * doubled[None, :]) % (2 * length))
        seeds += [np.cos(angle), np.sin(angle)]
    return [np.asarray(a, np.float32) for a in seeds]


def packed(state, to_modes, from_modes, mode_depth):
    wide, lev = lax.axis_size("wide"), lax.axis_size("lev")
    levels, rows, cols = state.shape
    devices = wide * lev
    length = cols + E
    half = length // 2
    chunks = 2 * KT // (devices * STEP)
    width = devices * 8
    tail = rows - LANES
    extra = E // wide
    block = levels * STEP + dense_rows(tail)[0]
    total = lev * levels
    f32, bf16 = jnp.float32, jnp.bfloat16

    starts = np.arange(wide // 2)[:, None]
    order = np.concatenate(
        [
            (starts * rows + np.arange(LANES)).reshape(-1),
            np.concatenate(
                [starts * rows + LANES + np.arange(tail), cols + starts * extra + np.arange(extra)], axis=1
            ).reshape(-1),
        ]
    )
    seeds_x = wave_seeds(2 * np.arange(half) + 1, length)
    seeds_y = wave_seeds(2 * order - (cols - 1), length)
    weights = edge_weights(E)
    edge_x = np.concatenate([np.zeros((4, HALF), np.float32), weights], axis=1)
    edge_y = np.zeros((2, 4, half), np.float32)
    outside = order >= cols
    ahead, behind = weights[:, order[outside] - cols], weights[:, E - 1 - (order[outside] - cols)]
    edge_y[0][:, outside], edge_y[1][:, outside] = ahead + behind, ahead - behind
    edge_y = edge_y[:, :, wide // 2 * LANES :]
    waves = np.arange(KT)
    lap = 4.0 * np.sin(np.pi * waves / length) ** 2
    facts = np.stack([lap, waves * waves, np.where(waves == 0, 1.0, 2.0)]).astype(np.float32)
    own = np.zeros((3, STEP, LANES), np.float32)
    own[:, :, : KT // 8] = np.tile(facts.reshape(3, -1, 8).transpose(0, 2, 1), (1, 2, 1))
    line = np.tile(facts, (1, 2))
    line[2] /= length * length

    wide_index = lax.axis_index("wide")
    place = jnp.stack([lax.rem(wide_index, 2), (wide_index >= wide // 2).astype(jnp.int32)])
    me = (wide_index * lev + lax.axis_index("lev")).reshape(1)
    smem = pl.BlockSpec(memory_space=pltpu.SMEM)
    vmem = pl.BlockSpec(memory_space=pltpu.VMEM)
    anywhere = pl.BlockSpec(memory_space=pl.ANY)
    table = (KT, half)

    def params(mib):
        return pltpu.CompilerParams(vmem_limit_bytes=mib << 20)

    def whole(a):
        return pl.BlockSpec(a.shape, lambda i: (0,) * a.ndim)

    def cost(flops, size):
        return pl.CostEstimate(flops=flops, bytes_accessed=size, transcendentals=0)

    def hbm(a):
        return pltpu.with_memory_space_constraint(a, pltpu.HBM)

    def to_columns(chunk):
        operands = [hbm(jnp.asarray(a)) for a in (edge_x, *seeds_x)]
        size = LANES + HALF
        return pl.pallas_call(
            functools.partial(forward_x, chunk),
            grid=(levels,),
            in_specs=[smem, anywhere] + [whole(a) for a in operands],
            out_specs=pl.BlockSpec((devices * block, LANES), lambda i: (0, 0)),
            out_shape=jax.ShapeDtypeStruct((devices * block, LANES), f32),
            scratch_shapes=[
                *[pltpu.VMEM((width, half), bf16)] * 4,
                *[pltpu.VMEM((2 * size, half), bf16)] * 2,
                pltpu.VMEM(state.shape, f32),
                pltpu.VMEM((devices, STEP + STEP // 2, LANES), f32),
                pltpu.SemaphoreType.DMA((levels,)),
            ],
            compiler_params=params(LIMITS[0]),
            cost_estimate=cost(12 * width * levels * size * half, 8 << 20),
            name=f"forward_x_{chunk}",
        )(place, hbm(state), *operands)

    def all_tables(after):
        operands = [hbm(jnp.asarray(a)) for a in (*seeds_x, *seeds_y)]
        steps = KT // TILE
        return pl.pallas_call(
            make_tables,
            grid=(steps,),
            in_specs=[anywhere] + [whole(a) for a in operands],
            out_specs=[pl.BlockSpec((TILE, half), lambda i: (i, 0))] * 4
            + [pl.BlockSpec((2, TILE, half), lambda i: (0, i, 0))] * 2,
            out_shape=[pltpu.HBM(table, bf16)] * 4 + [pltpu.HBM((2, *table), bf16)] * 2,
            compiler_params=params(LIMITS[1]),
            cost_estimate=cost(32 * KT * half, 8 << 20),
            name="make_tables",
        )(after, *operands)

    def through(chunk, got, high, low):
        operands = [got, hbm(high), hbm(low), *(jnp.asarray(a) for a in (edge_y, own, line))]
        span = total * STEP
        return pl.pallas_call(
            functools.partial(middle, chunk, devices, wide=wide, tail=tail),
            in_specs=[smem] * 4 + [vmem] * len(operands),
            out_specs=vmem,
            out_shape=jax.ShapeDtypeStruct(got.shape, f32),
            scratch_shapes=[
                pltpu.VMEM((2, 2 * span, half), bf16),
                pltpu.VMEM((2 * span, 2 * KT), bf16),
                pltpu.VMEM((span, LANES), f32),
                *[pltpu.VMEM((devices, (levels + 1) * STEP + STEP // 2, LANES), f32)] * 2,
            ],
            compiler_params=params(LIMITS[2]),
            cost_estimate=cost(24 * span * KT * half, 6 << 20),
            name=f"middle_{chunk}",
        )(me, to_modes, from_modes, mode_depth, *operands)

    def to_rows(chunk, got, tables, prior):
        size = LANES + HALF
        sums = pl.BlockSpec((1, rows, cols), lambda i: (i, 0, 0))
        more = prior is not None
        return pl.pallas_call(
            functools.partial(inverse_x, chunk, more=more),
            grid=(levels,),
            in_specs=[smem, whole(got)] + [anywhere] * 4 + [sums] * more,
            out_specs=sums,
            out_shape=pltpu.HBM(state.shape, f32) if not more else jax.ShapeDtypeStruct(state.shape, f32),
            scratch_shapes=[
                pltpu.VMEM((2, 2 * size, width), bf16),
                pltpu.VMEM((2, levels, HALF, width), f32),
                *[pltpu.VMEM((width, half), bf16)] * 4,
                pltpu.VMEM((devices, STEP + STEP // 2, LANES), f32),
                pltpu.SemaphoreType.DMA((4,)),
            ],
            compiler_params=params(LIMITS[3]),
            cost_estimate=cost(12 * width * levels * size * half, 8 << 20),
            name=f"inverse_x_{chunk}",
        )(place, got, *map(hbm, tables), *([hbm(prior)] if more else []))

    def exchange(sent):
        return lax.all_to_all(sent.reshape(-1, 1, LANES), AXES, 0, 0, tiled=True).reshape(sent.shape)

    sent = [to_columns(chunk) for chunk in range(chunks)]
    tables = all_tables(sent[-1])
    high, low = (a.reshape(2 * KT, half) for a in tables[4:])
    arrived = [exchange(part) for part in sent]
    returned = [exchange(through(chunk, got, high, low)) for chunk, got in enumerate(arrived)]
    value = None
    for chunk, got in enumerate(returned):
        value = to_rows(chunk, got, tables[:4], value)
    return value


def solution(mesh):
    placed = (P("lev", "wide", None), P(), P(), P())

    def shards(state, *rest):
        fits = packs(lax.axis_size("wide"), lax.axis_size("lev"), *state.shape)
        return (packed if fits else plain)(state, *rest)

    return jax.shard_map(
        shards, mesh=mesh, in_specs=placed, out_specs=P("lev", "wide", None), check_vma=False
    )
```

```python
import functools

import jax
import jax.numpy as jnp
import numpy as np
from jax import lax
from jax.experimental import pallas as pl
from jax.experimental.pallas import tpu as pltpu
from jax.sharding import PartitionSpec as P

I = 1472
E = 64
KT = 512
STEP = 16
LANES = 128
HALF = 64
TILE = 256

HIGH = lax.Precision.HIGH
HIGHEST = lax.Precision.HIGHEST
AXES = ("wide", "lev")


def blend_weights(extra):
    f = (np.arange(extra, dtype=np.float64) + 1.0) / (extra + 1.0)
    f2, f3 = f * f, f * f * f
    return 2 * f3 - 3 * f2 + 1, f3 - 2 * f2 + f, -2 * f3 + 3 * f2, f3 - f2


def edge_weights(extra):
    h00, h10, h01, h11 = blend_weights(extra)
    return np.stack([h01 - h11, h11, -h10, h00 + h10]).astype(np.float32)


def extend(block, extra):
    w = jnp.asarray(edge_weights(extra))
    added = (
        block[..., :1] * w[0] + block[..., 1:2] * w[1] + block[..., -2:-1] * w[2] + block[..., -1:] * w[3]
    )
    return jnp.concatenate([block, added], axis=-1)


def cas_seeds(waves, positions, length):
    turn = 2.0 * np.pi / length
    base = waves[::STEP].astype(np.int64)
    coarse = turn * ((base[:, None] * positions[None, :]) % length)
    fine = turn * ((np.arange(STEP)[:, None] * positions[None, :]) % length)
    parts = np.cos(coarse) + np.sin(coarse), np.cos(coarse) - np.sin(coarse), np.cos(fine), np.sin(fine)
    return [np.asarray(a, np.float32) for a in parts]


def cas_table(waves, positions, length):
    plus, minus, cosine, sine = (jnp.asarray(a) for a in cas_seeds(waves, positions, length))
    table = plus[:, None, :] * cosine[None] + minus[:, None, :] * sine[None]
    return table.reshape(len(waves), len(positions))


def plain(state, to_modes, from_modes, mode_depth):
    wide, lev = lax.axis_size("wide"), lax.axis_size("lev")
    devices = wide * lev
    levels, rows, cols = state.shape
    length = I + E
    waves = np.arange(-KT, KT)
    share = len(waves) // devices
    table = cas_table(waves, np.arange(length), length)
    spec = jnp.einsum("qn,lrn->qlr", table, extend(state, E), precision=HIGH)
    spec = spec.reshape(devices, share, levels * rows)
    spec = lax.all_to_all(spec, AXES, 0, 0, tiled=True)
    spec = spec.reshape(wide, lev, share, levels, rows).transpose(1, 3, 2, 0, 4)
    spec = extend(spec.reshape(lev * levels, share, wide * rows), E)
    spec = jnp.einsum("lqr,pr->lqp", spec, table, precision=HIGH)
    first = (lax.axis_index("wide") * lev + lax.axis_index("lev")) * share
    lap = (4.0 * np.sin(np.pi * waves / length) ** 2).astype(np.float32)
    square = (waves * waves).astype(np.int32)
    lap_q = lax.dynamic_slice_in_dim(jnp.asarray(lap), first, share)
    square_q = lax.dynamic_slice_in_dim(jnp.asarray(square), first, share)
    keep = (square_q[:, None] + square[None, :] < KT * KT).astype(jnp.float32)
    modes = jnp.einsum("ml,lqp->mqp", to_modes, spec, precision=HIGHEST)
    solved = modes * keep / (1.0 + mode_depth[:, None, None] * (lap_q[:, None] + lap[None, :]))
    mixed = jnp.einsum("lm,mqp->lqp", from_modes, solved, precision=HIGHEST)
    back = jnp.einsum("lqp,pr->lqr", mixed, table[:, :I], precision=HIGH)
    back = back.reshape(lev, levels, share, wide, rows).transpose(3, 0, 2, 1, 4)
    back = lax.all_to_all(back.reshape(devices, share, levels * rows), AXES, 0, 0, tiled=True)
    back = back.reshape(len(waves), levels, rows)
    return jnp.einsum("qlr,qn->lrn", back, table[:, :I], precision=HIGH) / (length * length)


LIMITS = (16, 16, 20, 16)


def split(value):
    high = value.astype(jnp.bfloat16)
    return high, (value - high.astype(jnp.float32)).astype(jnp.bfloat16)


def dot(a, b, contract):
    return lax.dot_general(a, b, (contract, ((), ())), preferred_element_type=jnp.float32)


def left_half():
    return lax.broadcasted_iota(jnp.int32, (1, LANES), 1) < HALF


def swap(value):
    return pltpu.roll(value, HALF, 1)


def mirror(value):
    order = LANES - 1 - lax.broadcasted_iota(jnp.int32, value.shape, 1)
    return jnp.take_along_axis(value, order, axis=1)


def empty_lanes(upper, rest):
    lane = lax.broadcasted_iota(jnp.int32, (1, LANES), 1) + rest * upper
    return lax.rem(lane, HALF) >= rest


def dense_rows(rest):
    lasting = STEP + STEP // 2
    return lasting - lasting * (HALF - rest) // HALF, HALF - rest


def fold_rows(read, write, empty, rest):
    kept, gap = dense_rows(rest)
    each = rest // gap
    for j in range(kept):
        moved = pltpu.roll(read(kept + j // each), rest - gap * (j % each), 1)
        write(j, jnp.where(empty, moved, read(j)))


def unfold_rows(read, write, empty, rest):
    kept, gap = dense_rows(rest)
    each = rest // gap
    for i in range(kept // each):
        back = 0.0
        for j in range(i * each, (i + 1) * each):
            value = read(j)
            write(j, jnp.where(empty, 0.0, value))
            back = back + pltpu.roll(jnp.where(empty, value, 0.0), LANES - rest + gap * (j % each), 1)
        write(kept + i, back)


def at(start, size, unit):
    return pl.ds(start if isinstance(start, int) else pl.multiple_of(start, unit), size)


def fill_tables(seeds, first, cos_high, cos_low, sin_high, sin_low):
    coarse_cos, coarse_sin, fine_cos, fine_sin = seeds
    for lane in range(0, cos_high.shape[-1], TILE):
        lanes = slice(lane, lane + TILE)
        fine_c, fine_s = fine_cos[:, lanes], fine_sin[:, lanes]
        for group in range(cos_high.shape[0] // STEP):
            rows = slice(group * STEP, (group + 1) * STEP)
            pick = pl.ds(first + group, 1)
            coarse_c, coarse_s = coarse_cos[pick, lanes], coarse_sin[pick, lanes]
            cos_high[rows, lanes], cos_low[rows, lanes] = split(coarse_c * fine_c - coarse_s * fine_s)
            sin_high[rows, lanes], sin_low[rows, lanes] = split(coarse_s * fine_c + coarse_c * fine_s)


def make_tables(order, *refs):
    seeds_x, seeds_y, tables_x, (high, low) = refs[:4], refs[4:8], refs[8:12], refs[12:]
    first = pl.program_id(0) * (tables_x[0].shape[0] // STEP)
    fill_tables(seeds_x, first, *tables_x)
    fill_tables(seeds_y, first, high.at[0], low.at[0], high.at[1], low.at[1])


def forward_x(chunk, place, x, edge, *refs):
    seeds, (out, *tables, even, uneven, buffer, packed, in_sems) = refs[:4], refs[4:]
    levels, rows, cols = x.shape
    waves = tables[0].shape[0]
    groups = waves // 8
    size = LANES + HALF
    half = tables[0].shape[1]
    odd, upper = place[0], place[1]
    rest = rows - LANES
    block = 32

    def fetch(level):
        return pltpu.make_async_copy(x.at[level], buffer.at[level], in_sems.at[level])

    height = out.shape[0] // groups

    for level in range(levels):
        fetch(level).start()
    fill_tables(seeds, chunk * (waves // STEP), *tables)

    for level in range(levels):
        fetch(level).wait()
        for r in range(0, size, block):

            def read(lanes):
                if r < LANES:
                    return buffer[level, at(rest * upper + r, block, 8), lanes]
                first = r - LANES
                live = min(block, rest - first)
                low = buffer[level, LANES + first : LANES + first + live, lanes]
                if live < block:
                    low = jnp.concatenate([low, jnp.zeros((block - live, low.shape[1]), low.dtype)], axis=0)
                shift = HALF - rest
                if first < shift:
                    high = buffer[level, 0 : block - shift, lanes]
                    high = jnp.concatenate([jnp.zeros((shift, high.shape[1]), high.dtype), high], axis=0)
                else:
                    high = buffer[level, first - shift : first - shift + block, lanes]
                return jnp.where(upper == 1, high, low)

            where = slice(r, r + block)
            above = slice(size + r, size + r + block)
            for tile in range(half // LANES):
                lanes = slice(tile * LANES, (tile + 1) * LANES)
                value = read(lanes)
                start = cols + HALF - (tile + 1) * LANES
                other = read(slice(start, min(start + LANES, cols)))
                if tile == 0:
                    ends = (value[:, 0:1], value[:, 1:2], other[:, HALF - 2 : HALF - 1], other[:, HALF - 1 : HALF])
                    other = jnp.concatenate([other, jnp.zeros_like(other)], axis=1)
                    for i, end in enumerate(ends):
                        other = other + end * edge[i : i + 1]
                other = mirror(other)
                even[where, lanes], even[above, lanes] = split(value + other)
                uneven[where, lanes], uneven[above, lanes] = split(value - other)

        across = ((1,), (1,))
        blank = jnp.zeros((HALF, waves), jnp.float32)
        for part, (source, high, low) in enumerate(((even, *tables[:2]), (uneven, *tables[2:]))):
            both = dot(source[...], high[...], across)
            spec = both[:size] + (both[size:] + dot(source[:size], low[...], across))
            full = spec[:LANES].T
            first = level * STEP + part * 8
            for d in range(groups):
                out[d * height + first : d * height + first + 8] = full[d * 8 : d * 8 + 8]
            if level < 2:
                first = part * 8
                if level == 0:
                    turned = jnp.concatenate([spec[LANES:], blank], axis=0).T
                    packed[:, first : first + 8] = turned.reshape(groups, 8, LANES)
                else:
                    turned = jnp.concatenate([blank, spec[LANES:]], axis=0).T
                    value = packed[:, first : first + 8].reshape(waves, LANES) + turned
                    value = jnp.where(odd == 1, swap(value), value)
                    packed[:, first : first + 8] = value.reshape(groups, 8, LANES)
            else:
                pieces = [spec[LANES:], blank] if part == 0 else [blank, spec[LANES:]]
                turned = jnp.concatenate(pieces, axis=0).T.reshape(groups, 8, LANES)
                first = STEP
                if part == 0:
                    packed[:, first : first + 8] = turned
                else:
                    packed[:, first : first + 8] = packed[:, first : first + 8] + turned

    def write(j, value):
        out[pl.ds(levels * STEP + j, groups, stride=height)] = value

    fold_rows(lambda j: packed[:, j], write, empty_lanes(upper, rest), rest)


def middle(
    chunk, devices, me, to_modes, from_modes, depth, arrived, *refs, wide, tail
):
    high, low, edge, own, line, leaving, xs, ms, ends, got, out = refs
    count = got.shape[0]
    lev = count // wide
    total = to_modes.shape[0]
    levels = total // lev
    span = total * STEP
    pairs = wide // 2
    left = left_half()
    rem = slice(levels * STEP, (levels + 1) * STEP)
    rem2 = slice((levels + 1) * STEP, (levels + 1) * STEP + STEP // 2)
    half = high.shape[1]
    waves = high.shape[0] // 2

    def rows_of(lv, level):
        start = (lv * levels + level) * STEP
        return start, slice(start, start + STEP)

    height = arrived.shape[0] // count
    block_index = lax.broadcasted_iota(jnp.int32, (count, 1), 0)
    empty = empty_lanes((block_index >= count // 2).astype(jnp.int32), tail)
    fulls = levels * STEP
    for d in range(count):
        got[d, :fulls] = arrived[d * height : d * height + fulls]

    def keep_row(j, value):
        got[:, fulls + j] = value

    def send_row(j, value):
        leaving[pl.ds(fulls + j, count, stride=height)] = value

    unfold_rows(lambda j: arrived[pl.ds(fulls + j, count, stride=height)], keep_row, empty, tail)

    for lv in range(lev):
        for level in range(levels):
            rows = rows_of(lv, level)[1]
            full = slice(level * STEP, (level + 1) * STEP)
            ends[rows, 0:2] = got[lv, full, 0:2]
            ends[rows, 2:4] = got[(wide - 1) * lev + lv, full, LANES - 2 : LANES]

    def put(part, start, lanes, value):
        for base, piece in zip((0, span), split(value)):
            xs[part, base + start : base + start + value.shape[0], lanes] = piece

    def gather(pair, carry):
        weights = edge[:, :, at(pair * LANES, LANES, LANES)]
        for lv in range(lev):
            a, b = 2 * pair, 2 * pair + 1
            low_a, low_b = a * lev + lv, b * lev + lv
            top_a, top_b = (wide - 1 - a) * lev + lv, (wide - 1 - b) * lev + lv
            for level in range(levels):
                start = rows_of(lv, level)[0]
                full = slice(level * STEP, (level + 1) * STEP)
                for w, src, top in ((a, low_a, top_a), (b, low_b, top_b)):
                    value, other = got[src, full], mirror(got[top, full])
                    lanes = at(w * LANES, LANES, LANES)
                    put(0, start, lanes, value + other)
                    put(1, start, lanes, value - other)
            turned = mirror(got[top_a, rem]), mirror(got[top_b, rem])
            turned2 = swap(mirror(got[top_a, rem2])), swap(mirror(got[top_b, rem2]))
            for part, sign in ((0, 1.0), (1, -1.0)):
                fa, fb = got[low_a, rem] + sign * turned[0], got[low_b, rem] + sign * turned[1]
                ga, gb = got[low_a, rem2] + sign * turned2[0], got[low_b, rem2] + sign * turned2[1]
                values = (
                    jnp.where(left, fa, fb),
                    swap(jnp.where(left, fb, fa)),
                    jnp.concatenate([jnp.where(left, ga, swap(gb)), jnp.where(left, swap(ga), gb)], axis=0),
                )
                for level, value in enumerate(values):
                    start, rows = rows_of(lv, level)
                    for i in range(4):
                        value = value + ends[rows, i : i + 1] * weights[part, i : i + 1]
                    put(part, start, at(pairs * LANES + pair * LANES, LANES, LANES), value)
        return carry

    lax.fori_loop(0, pairs // 2, gather, 0)

    group = chunk * devices + me[0]
    mine = lax.broadcasted_iota(jnp.int32, (1, LANES), 1) == group
    lap_q, square_q, weight_q = (
        jnp.sum(jnp.where(mine, own[i], 0.0), axis=1, keepdims=True) for i in range(3)
    )

    def solve(tile, carry):
        where = at(tile * TILE, TILE, TILE)
        part = tile // (waves // TILE)
        across = ((1,), (1,))
        both = dot(xs[part], high[where], across)
        spec = both[:span] + (both[span:] + dot(xs[part, :span], low[where], across))
        for piece in range(TILE // LANES):
            lanes = slice(piece * LANES, (piece + 1) * LANES)
            here = at(tile * TILE + piece * LANES, LANES, LANES)
            lap = lap_q + line[0:1, here]
            scale = jnp.where(square_q + line[1:2, here] < float(KT * KT), weight_q * line[2:3, here], 0.0)
            parts = [spec[l * STEP : (l + 1) * STEP, lanes] for l in range(total)]
            solved = []
            for m in range(total):
                mode = sum(to_modes[m, l] * parts[l] for l in range(total))
                solved.append(mode * scale / (1.0 + depth[m] * lap))
            for l in range(total):
                mixed = sum(from_modes[l, m] * solved[m] for m in range(total))
                for base, value in zip((0, span), split(mixed)):
                    ms[base + l * STEP : base + (l + 1) * STEP, here] = value
        return carry

    lax.fori_loop(0, 2 * waves // TILE, solve, 0)

    def back(start):
        where = at(start, TILE, TILE)
        down = ((1,), (0,))
        sums = []
        for part in range(2):
            k = slice(part * waves, (part + 1) * waves)
            both = dot(ms[:, k], high[k, where], down)
            sums.append(both[:span] + (both[span:] + dot(ms[:span, k], low[k, where], down)))
        return sums[0] + sums[1], sums[0] - sums[1]

    def scatter(pair, carry):
        values = back(pair * TILE)
        for piece in range(2):
            w = 2 * pair + piece
            lanes = slice(piece * LANES, (piece + 1) * LANES)
            for lv in range(lev):
                for level in range(levels):
                    rows = rows_of(lv, level)[1]
                    full = slice(level * STEP, (level + 1) * STEP)
                    out[w * lev + lv, full] = values[0][rows, lanes]
                    out[(wide - 1 - w) * lev + lv, full] = mirror(values[1][rows, lanes])
        return carry

    lax.fori_loop(0, pairs // 2, scatter, 0)

    for quad in range(pairs // 4):
        values = back(pairs * LANES + quad * TILE)
        for piece in range(2):
            pair = 2 * quad + piece
            lanes = slice(piece * LANES, (piece + 1) * LANES)
            for lv in range(lev):
                packs_of = []
                for value in values:
                    zero, one, two = (value[rows_of(lv, level)[1], lanes] for level in range(3))
                    one = swap(one)
                    cos, sin = two[: STEP // 2], two[STEP // 2 :]
                    packs_of.append(
                        (
                            (jnp.where(left, zero, one), jnp.where(left, cos, swap(sin))),
                            (jnp.where(left, one, zero), jnp.where(left, swap(cos), sin)),
                        )
                    )
                for i in range(2):
                    w = 2 * pair + i
                    out[w * lev + lv, rem], out[w * lev + lv, rem2] = packs_of[0][i]
                    top = (wide - 1 - w) * lev + lv
                    out[top, rem], out[top, rem2] = mirror(packs_of[1][i][0]), swap(mirror(packs_of[1][i][1]))

    for d in range(count):
        leaving[d * height : d * height + fulls] = out[d, :fulls]
    fold_rows(lambda j: out[:, fulls + j], send_row, empty, tail)


def inverse_x(chunk, place, arrived, *refs, more):
    sources, refs = refs[:4], refs[4:]
    prior, refs = (refs[0], refs[1:]) if more else (None, refs)
    final, got, out, zs, rems, *tables, unpacked, sems, sent_sems = refs
    levels, rows, cols = out.shape
    waves, half = tables[0].shape
    size = LANES + HALF
    odd, upper = place[0], place[1]
    rest = rows - LANES
    groups = waves // 8
    height = got.shape[0] // groups

    copies = [(arrived, got)]
    copies += [(source.at[pl.ds(chunk * waves, waves)], target) for source, target in zip(sources, tables)]
    copies += [(prior.at[level], out.at[level]) for level in range(levels)] if more else []
    fetches = [pltpu.make_async_copy(*pair, sems.at[i]) for i, pair in enumerate(copies)]
    for fetch in fetches:
        fetch.start()

    def turn(start, part):
        first = start + part * 8
        return jnp.concatenate([got[pl.ds(first + d * height, 8)] for d in range(groups)], axis=0).T

    def keep_row(j, value):
        unpacked[:, j] = value

    fetches[0].wait()
    unfold_rows(
        lambda j: got[pl.ds(levels * STEP + j, groups, stride=height)], keep_row, empty_lanes(upper, rest), rest
    )
    last = unpacked[:, STEP:].reshape(waves, LANES).T
    for part in range(2):
        value = unpacked[:, part * 8 : part * 8 + 8].reshape(waves, LANES).T
        for i in range(2):
            rems[part, i] = value[i * HALF : (i + 1) * HALF]
        rems[part, 2] = last[part * HALF : (part + 1) * HALF]

    down = ((1,), (0,))
    shift = HALF - rest
    sends = []

    def send(level, lanes):
        copy = pltpu.make_async_copy(out.at[level, :, lanes], final.at[level, :, lanes], sent_sems.at[len(sends)])
        copy.start()
        sends.append(copy)

    for level in range(levels):
        which = (odd, 1 - odd, 2)[level]
        for part in range(2):
            value = turn(level * STEP, part)
            for base, piece in zip((0, size), split(value)):
                zs[level, part, base : base + LANES] = piece
            for base, piece in zip((0, size), split(rems[part, which])):
                zs[level, part, base + LANES : base + size] = piece
        if level == 0:
            for fetch in fetches[1:5]:
                fetch.wait()
        if more:
            fetches[5 + level].wait()

        def store(lanes, value):
            full, tail = value[:LANES], value[LANES:]
            tail = jnp.where(upper == 1, tail[shift:], tail[:rest])
            for start, piece in ((rest * upper, full), (LANES * (1 - upper), tail)):
                where = at(start, piece.shape[0], 8)
                out[level, where, lanes] = piece + out[level, where, lanes] if more else piece

        for tile in range(half // TILE):
            where = slice(tile * TILE, (tile + 1) * TILE)
            sums = []
            for part in range(2):
                high, low = tables[2 * part], tables[2 * part + 1]
                both = dot(zs[level, part], high[:, where], down)
                sums.append(both[:size] + (both[size:] + dot(zs[level, part, :size], low[:, where], down)))
            store(where, sums[0] + sums[1])
            other = sums[0] - sums[1]
            for piece in range(TILE // LANES):
                start = 2 * half - tile * TILE - (piece + 1) * LANES
                end = min(start + LANES, cols)
                store(slice(start, end), mirror(other[:, piece * LANES : (piece + 1) * LANES])[:, : end - start])
            if level == levels - 1:
                send(level, pl.ds(tile * TILE, TILE))
                start = 2 * half - (tile + 1) * TILE
                send(level, pl.ds(start, min(start + TILE, cols) - start))
        if level < levels - 1:
            send(level, pl.ds(0, cols))
    for copy in sends:
        copy.wait()


def packs(wide, lev, levels, rows, cols):
    share = 2 * KT // (wide * lev)
    return (
        levels == 3
        and wide % 8 == 0
        and LANES < rows <= LANES + HALF
        and rows % 8 == 0
        and (LANES + HALF - rows) * wide == E
        and cols % LANES == HALF == E
        and (cols + E) % (2 * TILE) == 0
        and (wide * lev * 8) % TILE == 0
        and share % STEP == 0
        and (STEP + STEP // 2) * (LANES + HALF - rows) % HALF == 0
        and (rows - LANES) % (LANES + HALF - rows) == 0
        and KT // 8 <= LANES
    )


def wave_seeds(doubled, length):
    turn = np.pi / length
    seeds = []
    for waves in (np.arange(0, KT, STEP), np.arange(STEP)):
        angle = turn * ((waves[:, None] * doubled[None, :]) % (2 * length))
        seeds += [np.cos(angle), np.sin(angle)]
    return [np.asarray(a, np.float32) for a in seeds]


def packed(state, to_modes, from_modes, mode_depth):
    wide, lev = lax.axis_size("wide"), lax.axis_size("lev")
    levels, rows, cols = state.shape
    devices = wide * lev
    length = cols + E
    half = length // 2
    chunks = 2 * KT // (devices * STEP)
    width = devices * 8
    tail = rows - LANES
    extra = E // wide
    block = levels * STEP + dense_rows(tail)[0]
    total = lev * levels
    f32, bf16 = jnp.float32, jnp.bfloat16

    starts = np.arange(wide // 2)[:, None]
    order = np.concatenate(
        [
            (starts * rows + np.arange(LANES)).reshape(-1),
            np.concatenate(
                [starts * rows + LANES + np.arange(tail), cols + starts * extra + np.arange(extra)], axis=1
            ).reshape(-1),
        ]
    )
    seeds_x = wave_seeds(2 * np.arange(half) + 1, length)
    seeds_y = wave_seeds(2 * order - (cols - 1), length)
    weights = edge_weights(E)
    edge_x = np.concatenate([np.zeros((4, HALF), np.float32), weights], axis=1)
    edge_y = np.zeros((2, 4, half), np.float32)
    outside = order >= cols
    ahead, behind = weights[:, order[outside] - cols], weights[:, E - 1 - (order[outside] - cols)]
    edge_y[0][:, outside], edge_y[1][:, outside] = ahead + behind, ahead - behind
    edge_y = edge_y[:, :, wide // 2 * LANES :]
    waves = np.arange(KT)
    lap = 4.0 * np.sin(np.pi * waves / length) ** 2
    facts = np.stack([lap, waves * waves, np.where(waves == 0, 1.0, 2.0)]).astype(np.float32)
    own = np.zeros((3, STEP, LANES), np.float32)
    own[:, :, : KT // 8] = np.tile(facts.reshape(3, -1, 8).transpose(0, 2, 1), (1, 2, 1))
    line = np.tile(facts, (1, 2))
    line[2] /= length * length

    wide_index = lax.axis_index("wide")
    place = jnp.stack([lax.rem(wide_index, 2), (wide_index >= wide // 2).astype(jnp.int32)])
    me = (wide_index * lev + lax.axis_index("lev")).reshape(1)
    smem = pl.BlockSpec(memory_space=pltpu.SMEM)
    vmem = pl.BlockSpec(memory_space=pltpu.VMEM)
    anywhere = pl.BlockSpec(memory_space=pl.ANY)
    table = (KT, half)

    def params(mib):
        return pltpu.CompilerParams(vmem_limit_bytes=mib << 20)

    def whole(a):
        return pl.BlockSpec(a.shape, lambda i: (0,) * a.ndim)

    def cost(flops, size):
        return pl.CostEstimate(flops=flops, bytes_accessed=size, transcendentals=0)

    def hbm(a):
        return pltpu.with_memory_space_constraint(a, pltpu.HBM)

    def to_columns(chunk):
        operands = [hbm(jnp.asarray(a)) for a in (edge_x, *seeds_x)]
        size = LANES + HALF
        return pl.pallas_call(
            functools.partial(forward_x, chunk),
            grid=(1,),
            in_specs=[smem, anywhere] + [whole(a) for a in operands],
            out_specs=pl.BlockSpec((devices * block, LANES), lambda i: (0, 0)),
            out_shape=jax.ShapeDtypeStruct((devices * block, LANES), f32),
            scratch_shapes=[
                *[pltpu.VMEM((width, half), bf16)] * 4,
                *[pltpu.VMEM((2 * size, half), bf16)] * 2,
                pltpu.VMEM(state.shape, f32),
                pltpu.VMEM((devices, STEP + STEP // 2, LANES), f32),
                pltpu.SemaphoreType.DMA((levels,)),
            ],
            compiler_params=params(LIMITS[0]),
            cost_estimate=cost(12 * width * levels * size * half, 8 << 20),
            name=f"forward_x_{chunk}",
        )(place, hbm(state), *operands)

    def all_tables(after):
        operands = [hbm(jnp.asarray(a)) for a in (*seeds_x, *seeds_y)]
        steps = KT // TILE
        return pl.pallas_call(
            make_tables,
            grid=(steps,),
            in_specs=[anywhere] + [whole(a) for a in operands],
            out_specs=[pl.BlockSpec((TILE, half), lambda i: (i, 0))] * 4
            + [pl.BlockSpec((2, TILE, half), lambda i: (0, i, 0))] * 2,
            out_shape=[pltpu.HBM(table, bf16)] * 4 + [pltpu.HBM((2, *table), bf16)] * 2,
            compiler_params=params(LIMITS[1]),
            cost_estimate=cost(32 * KT * half, 8 << 20),
            name="make_tables",
        )(after, *operands)

    def through(chunk, got, high, low):
        operands = [got, hbm(high), hbm(low), *(jnp.asarray(a) for a in (edge_y, own, line))]
        span = total * STEP
        return pl.pallas_call(
            functools.partial(middle, chunk, devices, wide=wide, tail=tail),
            in_specs=[smem] * 4 + [vmem] * len(operands),
            out_specs=vmem,
            out_shape=jax.ShapeDtypeStruct(got.shape, f32),
            scratch_shapes=[
                pltpu.VMEM((2, 2 * span, half), bf16),
                pltpu.VMEM((2 * span, 2 * KT), bf16),
                pltpu.VMEM((span, LANES), f32),
                *[pltpu.VMEM((devices, (levels + 1) * STEP + STEP // 2, LANES), f32)] * 2,
            ],
            compiler_params=params(LIMITS[2]),
            cost_estimate=cost(24 * span * KT * half, 6 << 20),
            name=f"middle_{chunk}",
        )(me, to_modes, from_modes, mode_depth, *operands)

    def to_rows(chunk, got, tables, prior):
        size = LANES + HALF
        more = prior is not None
        return pl.pallas_call(
            functools.partial(inverse_x, chunk, more=more),
            in_specs=[smem] + [anywhere] * (5 + more),
            out_specs=anywhere,
            out_shape=jax.ShapeDtypeStruct(state.shape, f32) if more else pltpu.HBM(state.shape, f32),
            scratch_shapes=[
                pltpu.VMEM(got.shape, f32),
                pltpu.VMEM(state.shape, f32),
                pltpu.VMEM((levels, 2, 2 * size, width), bf16),
                pltpu.VMEM((2, levels, HALF, width), f32),
                *[pltpu.VMEM((width, half), bf16)] * 4,
                pltpu.VMEM((devices, STEP + STEP // 2, LANES), f32),
                pltpu.SemaphoreType.DMA((5 + levels,)),
                pltpu.SemaphoreType.DMA((levels - 1 + 2 * (half // TILE),)),
            ],
            compiler_params=params(LIMITS[3]),
            cost_estimate=cost(12 * width * levels * size * half, 8 << 20),
            name=f"inverse_x_{chunk}",
        )(place, got, *map(hbm, tables), *([hbm(prior)] if more else []))

    def exchange(sent):
        return lax.all_to_all(sent.reshape(-1, 1, LANES), AXES, 0, 0, tiled=True).reshape(sent.shape)

    sent = [to_columns(chunk) for chunk in range(chunks)]
    tables = all_tables(sent[-1])
    high, low = (a.reshape(2 * KT, half) for a in tables[4:])
    arrived = [exchange(part) for part in sent]
    returned = [exchange(through(chunk, got, high, low)) for chunk, got in enumerate(arrived)]
    value = None
    for chunk, got in enumerate(returned):
        value = to_rows(chunk, got, tables[:4], value)
    return value


def solution(mesh):
    placed = (P("lev", "wide", None), P(), P(), P())

    def shards(state, *rest):
        fits = packs(lax.axis_size("wide"), lax.axis_size("lev"), *state.shape)
        return (packed if fits else plain)(state, *rest)

    return jax.shard_map(
        shards, mesh=mesh, in_specs=placed, out_specs=P("lev", "wide", None), check_vma=False
    )
```

```python
import functools

import jax
import jax.numpy as jnp
import numpy as np
from jax import lax
from jax.experimental import pallas as pl
from jax.experimental.pallas import tpu as pltpu
from jax.sharding import PartitionSpec as P

I = 1472
E = 64
KT = 512
STEP = 16
LANES = 128
HALF = 64
TILE = 256

HIGH = lax.Precision.HIGH
HIGHEST = lax.Precision.HIGHEST
AXES = ("wide", "lev")


def blend_weights(extra):
    f = (np.arange(extra, dtype=np.float64) + 1.0) / (extra + 1.0)
    f2, f3 = f * f, f * f * f
    return 2 * f3 - 3 * f2 + 1, f3 - 2 * f2 + f, -2 * f3 + 3 * f2, f3 - f2


def edge_weights(extra):
    h00, h10, h01, h11 = blend_weights(extra)
    return np.stack([h01 - h11, h11, -h10, h00 + h10]).astype(np.float32)


def extend(block, extra):
    w = jnp.asarray(edge_weights(extra))
    added = (
        block[..., :1] * w[0] + block[..., 1:2] * w[1] + block[..., -2:-1] * w[2] + block[..., -1:] * w[3]
    )
    return jnp.concatenate([block, added], axis=-1)


def cas_seeds(waves, positions, length):
    turn = 2.0 * np.pi / length
    base = waves[::STEP].astype(np.int64)
    coarse = turn * ((base[:, None] * positions[None, :]) % length)
    fine = turn * ((np.arange(STEP)[:, None] * positions[None, :]) % length)
    parts = np.cos(coarse) + np.sin(coarse), np.cos(coarse) - np.sin(coarse), np.cos(fine), np.sin(fine)
    return [np.asarray(a, np.float32) for a in parts]


def cas_table(waves, positions, length):
    plus, minus, cosine, sine = (jnp.asarray(a) for a in cas_seeds(waves, positions, length))
    table = plus[:, None, :] * cosine[None] + minus[:, None, :] * sine[None]
    return table.reshape(len(waves), len(positions))


def plain(state, to_modes, from_modes, mode_depth):
    wide, lev = lax.axis_size("wide"), lax.axis_size("lev")
    devices = wide * lev
    levels, rows, cols = state.shape
    length = I + E
    waves = np.arange(-KT, KT)
    share = len(waves) // devices
    table = cas_table(waves, np.arange(length), length)
    spec = jnp.einsum("qn,lrn->qlr", table, extend(state, E), precision=HIGH)
    spec = spec.reshape(devices, share, levels * rows)
    spec = lax.all_to_all(spec, AXES, 0, 0, tiled=True)
    spec = spec.reshape(wide, lev, share, levels, rows).transpose(1, 3, 2, 0, 4)
    spec = extend(spec.reshape(lev * levels, share, wide * rows), E)
    spec = jnp.einsum("lqr,pr->lqp", spec, table, precision=HIGH)
    first = (lax.axis_index("wide") * lev + lax.axis_index("lev")) * share
    lap = (4.0 * np.sin(np.pi * waves / length) ** 2).astype(np.float32)
    square = (waves * waves).astype(np.int32)
    lap_q = lax.dynamic_slice_in_dim(jnp.asarray(lap), first, share)
    square_q = lax.dynamic_slice_in_dim(jnp.asarray(square), first, share)
    keep = (square_q[:, None] + square[None, :] < KT * KT).astype(jnp.float32)
    modes = jnp.einsum("ml,lqp->mqp", to_modes, spec, precision=HIGHEST)
    solved = modes * keep / (1.0 + mode_depth[:, None, None] * (lap_q[:, None] + lap[None, :]))
    mixed = jnp.einsum("lm,mqp->lqp", from_modes, solved, precision=HIGHEST)
    back = jnp.einsum("lqp,pr->lqr", mixed, table[:, :I], precision=HIGH)
    back = back.reshape(lev, levels, share, wide, rows).transpose(3, 0, 2, 1, 4)
    back = lax.all_to_all(back.reshape(devices, share, levels * rows), AXES, 0, 0, tiled=True)
    back = back.reshape(len(waves), levels, rows)
    return jnp.einsum("qlr,qn->lrn", back, table[:, :I], precision=HIGH) / (length * length)


LIMITS = (16, 16, 20, 16)


def split(value):
    high = value.astype(jnp.bfloat16)
    return high, (value - high.astype(jnp.float32)).astype(jnp.bfloat16)


def dot(a, b, contract):
    return lax.dot_general(a, b, (contract, ((), ())), preferred_element_type=jnp.float32)


def left_half():
    return lax.broadcasted_iota(jnp.int32, (1, LANES), 1) < HALF


def swap(value):
    return pltpu.roll(value, HALF, 1)


def mirror(value):
    order = LANES - 1 - lax.broadcasted_iota(jnp.int32, value.shape, 1)
    return jnp.take_along_axis(value, order, axis=1)


def put_rows(ref, start, value):
    height = ref.shape[0] * 8 // value.shape[0]
    for d in range(value.shape[0] // 8):
        ref[d * height + start : d * height + start + 8] = value[d * 8 : d * 8 + 8]


def get_rows(ref, start, count):
    height = ref.shape[0] // count
    return jnp.concatenate([ref[pl.ds(start + d * height, 8)] for d in range(count)], axis=0)


def strided(ref, start, count):
    height = ref.shape[0] // count

    def read(j):
        return ref[pl.ds(start + j, count, stride=height)]

    def write(j, value):
        ref[pl.ds(start + j, count, stride=height)] = value

    return read, write


def empty_lanes(upper, rest):
    lane = lax.broadcasted_iota(jnp.int32, (1, LANES), 1) + rest * upper
    return lax.rem(lane, HALF) >= rest


def dense_rows(rest):
    lasting = STEP + STEP // 2
    return lasting - lasting * (HALF - rest) // HALF, HALF - rest


def fold_rows(read, write, empty, rest):
    kept, gap = dense_rows(rest)
    each = rest // gap
    for j in range(kept):
        moved = pltpu.roll(read(kept + j // each), rest - gap * (j % each), 1)
        write(j, jnp.where(empty, moved, read(j)))


def unfold_rows(read, write, empty, rest):
    kept, gap = dense_rows(rest)
    each = rest // gap
    for i in range(kept // each):
        back = 0.0
        for j in range(i * each, (i + 1) * each):
            value = read(j)
            write(j, jnp.where(empty, 0.0, value))
            back = back + pltpu.roll(jnp.where(empty, value, 0.0), LANES - rest + gap * (j % each), 1)
        write(kept + i, back)


def at(start, size, unit):
    return pl.ds(start if isinstance(start, int) else pl.multiple_of(start, unit), size)


def fill_tables(seeds, first, cos_high, cos_low, sin_high, sin_low):
    coarse_cos, coarse_sin, fine_cos, fine_sin = seeds
    for lane in range(0, cos_high.shape[-1], TILE):
        lanes = slice(lane, lane + TILE)
        fine_c, fine_s = fine_cos[:, lanes], fine_sin[:, lanes]
        for group in range(cos_high.shape[0] // STEP):
            rows = slice(group * STEP, (group + 1) * STEP)
            pick = pl.ds(first + group, 1)
            coarse_c, coarse_s = coarse_cos[pick, lanes], coarse_sin[pick, lanes]
            cos_high[rows, lanes], cos_low[rows, lanes] = split(coarse_c * fine_c - coarse_s * fine_s)
            sin_high[rows, lanes], sin_low[rows, lanes] = split(coarse_s * fine_c + coarse_c * fine_s)


def make_tables(order, *refs):
    seeds_x, seeds_y, tables_x, (high, low) = refs[:4], refs[4:8], refs[8:12], refs[12:]
    first = pl.program_id(0) * (tables_x[0].shape[0] // STEP)
    fill_tables(seeds_x, first, *tables_x)
    fill_tables(seeds_y, first, high.at[0], low.at[0], high.at[1], low.at[1])


def forward_x(chunk, place, x, edge_in, *refs):
    sources, (out, *tables, even, uneven, buffer, packed), rest_refs = refs[:4], refs[4:13], refs[13:]
    edge, *seeds, in_sems, seed_sems = rest_refs
    levels, rows, cols = x.shape
    waves = tables[0].shape[0]
    groups = waves // 8
    size = LANES + HALF
    half = tables[0].shape[1]
    odd, upper = place[0], place[1]
    rest = rows - LANES
    block = 32

    def fetch(level):
        return pltpu.make_async_copy(x.at[level], buffer.at[level], in_sems.at[level])

    smalls = [
        pltpu.make_async_copy(source, target, seed_sems.at[i])
        for i, (source, target) in enumerate(zip((*sources, edge_in), (*seeds, edge)))
    ]
    for small in smalls:
        small.start()
    for level in range(levels):
        fetch(level).start()
    for small in smalls:
        small.wait()
    fill_tables(seeds, chunk * (waves // STEP), *tables)

    def reflect(level):
        fetch(level).wait()
        for r in range(0, size, block):

            def read(lanes):
                if r < LANES:
                    return buffer[level, at(rest * upper + r, block, 8), lanes]
                first = r - LANES
                live = min(block, rest - first)
                low = buffer[level, LANES + first : LANES + first + live, lanes]
                if live < block:
                    low = jnp.concatenate([low, jnp.zeros((block - live, low.shape[1]), low.dtype)], axis=0)
                shift = HALF - rest
                if first < shift:
                    high = buffer[level, 0 : block - shift, lanes]
                    high = jnp.concatenate([jnp.zeros((shift, high.shape[1]), high.dtype), high], axis=0)
                else:
                    high = buffer[level, first - shift : first - shift + block, lanes]
                return jnp.where(upper == 1, high, low)

            where = slice(r, r + block)
            above = slice(size + r, size + r + block)
            for tile in range(half // LANES):
                lanes = slice(tile * LANES, (tile + 1) * LANES)
                value = read(lanes)
                start = cols + HALF - (tile + 1) * LANES
                other = read(slice(start, min(start + LANES, cols)))
                if tile == 0:
                    ends = (value[:, 0:1], value[:, 1:2], other[:, HALF - 2 : HALF - 1], other[:, HALF - 1 : HALF])
                    other = jnp.concatenate([other, jnp.zeros_like(other)], axis=1)
                    for i, end in enumerate(ends):
                        other = other + end * edge[i : i + 1]
                other = mirror(other)
                even[level, where, lanes], even[level, above, lanes] = split(value + other)
                uneven[level, where, lanes], uneven[level, above, lanes] = split(value - other)

    def transform(level):
        across = ((1,), (1,))
        blank = jnp.zeros((HALF, waves), jnp.float32)
        for part, (source, high, low) in enumerate(((even, *tables[:2]), (uneven, *tables[2:]))):
            both = dot(source[level], high[...], across)
            spec = both[:size] + (both[size:] + dot(source[level, :size], low[...], across))
            full = spec[:LANES].T
            first = level * STEP + part * 8
            put_rows(out, first, full)
            if level < 2:
                first = part * 8
                if level == 0:
                    put_rows(packed, first, jnp.concatenate([spec[LANES:], blank], axis=0).T)
                else:
                    turned = jnp.concatenate([blank, spec[LANES:]], axis=0).T
                    value = get_rows(packed, first, groups) + turned
                    put_rows(packed, first, jnp.where(odd == 1, swap(value), value))
            elif part == 0:
                cosines = spec[LANES:]
            else:
                put_rows(packed, STEP, jnp.concatenate([cosines, spec[LANES:]], axis=0).T)

    reflect(0)
    for level in range(levels):
        if level + 1 < levels:
            reflect(level + 1)
        transform(level)
    fold_rows(
        strided(packed, 0, groups)[0], strided(out, levels * STEP, groups)[1], empty_lanes(upper, rest), rest
    )


def middle(
    chunk, devices, me, to_modes, from_modes, depth, arrived, *refs, wide, tail
):
    high, low, edge, own, line, leaving, xs, ms, ends, got, out = refs
    count = got.shape[0]
    lev = count // wide
    total = to_modes.shape[0]
    levels = total // lev
    span = total * STEP
    pairs = wide // 2
    left = left_half()
    rem = slice(levels * STEP, (levels + 1) * STEP)
    rem2 = slice((levels + 1) * STEP, (levels + 1) * STEP + STEP // 2)
    half = high.shape[1]
    waves = high.shape[0] // 2

    def rows_of(lv, level):
        start = (lv * levels + level) * STEP
        return start, slice(start, start + STEP)

    height = arrived.shape[0] // count
    block_index = lax.broadcasted_iota(jnp.int32, (count, 1), 0)
    empty = empty_lanes((block_index >= count // 2).astype(jnp.int32), tail)
    fulls = levels * STEP
    for d in range(count):
        got[d, :fulls] = arrived[d * height : d * height + fulls]

    def keep_row(j, value):
        got[:, fulls + j] = value

    def send_row(j, value):
        leaving[pl.ds(fulls + j, count, stride=height)] = value

    unfold_rows(lambda j: arrived[pl.ds(fulls + j, count, stride=height)], keep_row, empty, tail)

    for lv in range(lev):
        for level in range(levels):
            rows = rows_of(lv, level)[1]
            full = slice(level * STEP, (level + 1) * STEP)
            ends[rows, 0:2] = got[lv, full, 0:2]
            ends[rows, 2:4] = got[(wide - 1) * lev + lv, full, LANES - 2 : LANES]

    def put(part, start, lanes, value):
        for base, piece in zip((0, span), split(value)):
            xs[part, base + start : base + start + value.shape[0], lanes] = piece

    def gather(pair, carry):
        weights = edge[:, :, at(pair * LANES, LANES, LANES)]
        for lv in range(lev):
            a, b = 2 * pair, 2 * pair + 1
            low_a, low_b = a * lev + lv, b * lev + lv
            top_a, top_b = (wide - 1 - a) * lev + lv, (wide - 1 - b) * lev + lv
            for level in range(levels):
                start = rows_of(lv, level)[0]
                full = slice(level * STEP, (level + 1) * STEP)
                for w, src, top in ((a, low_a, top_a), (b, low_b, top_b)):
                    value, other = got[src, full], mirror(got[top, full])
                    lanes = at(w * LANES, LANES, LANES)
                    put(0, start, lanes, value + other)
                    put(1, start, lanes, value - other)
            turned = mirror(got[top_a, rem]), mirror(got[top_b, rem])
            turned2 = swap(mirror(got[top_a, rem2])), swap(mirror(got[top_b, rem2]))
            for part, sign in ((0, 1.0), (1, -1.0)):
                fa, fb = got[low_a, rem] + sign * turned[0], got[low_b, rem] + sign * turned[1]
                ga, gb = got[low_a, rem2] + sign * turned2[0], got[low_b, rem2] + sign * turned2[1]
                values = (
                    jnp.where(left, fa, fb),
                    swap(jnp.where(left, fb, fa)),
                    jnp.concatenate([jnp.where(left, ga, swap(gb)), jnp.where(left, swap(ga), gb)], axis=0),
                )
                for level, value in enumerate(values):
                    start, rows = rows_of(lv, level)
                    for i in range(4):
                        value = value + ends[rows, i : i + 1] * weights[part, i : i + 1]
                    put(part, start, at(pairs * LANES + pair * LANES, LANES, LANES), value)
        return carry

    lax.fori_loop(0, pairs // 2, gather, 0)

    group = chunk * devices + me[0]
    mine = lax.broadcasted_iota(jnp.int32, (1, LANES), 1) == group
    lap_q, square_q, weight_q = (
        jnp.sum(jnp.where(mine, own[i], 0.0), axis=1, keepdims=True) for i in range(3)
    )

    def solve(tile, carry):
        where = at(tile * TILE, TILE, TILE)
        part = tile // (waves // TILE)
        across = ((1,), (1,))
        both = dot(xs[part], high[where], across)
        spec = both[:span] + (both[span:] + dot(xs[part, :span], low[where], across))
        for piece in range(TILE // LANES):
            lanes = slice(piece * LANES, (piece + 1) * LANES)
            here = at(tile * TILE + piece * LANES, LANES, LANES)
            lap = lap_q + line[0:1, here]
            scale = jnp.where(square_q + line[1:2, here] < float(KT * KT), weight_q * line[2:3, here], 0.0)
            parts = [spec[l * STEP : (l + 1) * STEP, lanes] for l in range(total)]
            solved = []
            for m in range(total):
                mode = sum(to_modes[m, l] * parts[l] for l in range(total))
                solved.append(mode * scale / (1.0 + depth[m] * lap))
            for l in range(total):
                mixed = sum(from_modes[l, m] * solved[m] for m in range(total))
                for base, value in zip((0, span), split(mixed)):
                    ms[base + l * STEP : base + (l + 1) * STEP, here] = value
        return carry

    lax.fori_loop(0, 2 * waves // TILE, solve, 0)

    def back(start):
        where = at(start, TILE, TILE)
        down = ((1,), (0,))
        sums = []
        for part in range(2):
            k = slice(part * waves, (part + 1) * waves)
            both = dot(ms[:, k], high[k, where], down)
            sums.append(both[:span] + (both[span:] + dot(ms[:span, k], low[k, where], down)))
        return sums[0] + sums[1], sums[0] - sums[1]

    def scatter(pair, carry):
        values = back(pair * TILE)
        for piece in range(2):
            w = 2 * pair + piece
            lanes = slice(piece * LANES, (piece + 1) * LANES)
            for lv in range(lev):
                for level in range(levels):
                    rows = rows_of(lv, level)[1]
                    full = slice(level * STEP, (level + 1) * STEP)
                    out[w * lev + lv, full] = values[0][rows, lanes]
                    out[(wide - 1 - w) * lev + lv, full] = mirror(values[1][rows, lanes])
        return carry

    lax.fori_loop(0, pairs // 2, scatter, 0)

    for quad in range(pairs // 4):
        values = back(pairs * LANES + quad * TILE)
        for piece in range(2):
            pair = 2 * quad + piece
            lanes = slice(piece * LANES, (piece + 1) * LANES)
            for lv in range(lev):
                packs_of = []
                for value in values:
                    zero, one, two = (value[rows_of(lv, level)[1], lanes] for level in range(3))
                    one = swap(one)
                    cos, sin = two[: STEP // 2], two[STEP // 2 :]
                    packs_of.append(
                        (
                            (jnp.where(left, zero, one), jnp.where(left, cos, swap(sin))),
                            (jnp.where(left, one, zero), jnp.where(left, swap(cos), sin)),
                        )
                    )
                for i in range(2):
                    w = 2 * pair + i
                    out[w * lev + lv, rem], out[w * lev + lv, rem2] = packs_of[0][i]
                    top = (wide - 1 - w) * lev + lv
                    out[top, rem], out[top, rem2] = mirror(packs_of[1][i][0]), swap(mirror(packs_of[1][i][1]))

    for d in range(count):
        leaving[d * height : d * height + fulls] = out[d, :fulls]
    fold_rows(lambda j: out[:, fulls + j], send_row, empty, tail)


def inverse_x(chunk, place, arrived, *refs, more):
    sources, refs = refs[:4], refs[4:]
    prior, refs = (refs[0], refs[1:]) if more else (None, refs)
    final, got, out, zs, rems, *tables, unpacked, sems, sent_sems = refs
    levels, rows, cols = out.shape
    waves, half = tables[0].shape
    size = LANES + HALF
    odd, upper = place[0], place[1]
    rest = rows - LANES
    groups = waves // 8

    copies = [(arrived, got)]
    copies += [(source.at[pl.ds(chunk * waves, waves)], target) for source, target in zip(sources, tables)]
    copies += [(prior.at[level], out.at[level]) for level in range(levels)] if more else []
    fetches = [pltpu.make_async_copy(*pair, sems.at[i]) for i, pair in enumerate(copies)]
    for fetch in fetches:
        fetch.start()

    fetches[0].wait()
    unfold_rows(
        strided(got, levels * STEP, groups)[0], strided(unpacked, 0, groups)[1], empty_lanes(upper, rest), rest
    )
    last = get_rows(unpacked, STEP, groups).T
    for part in range(2):
        value = get_rows(unpacked, part * 8, groups).T
        for i in range(2):
            rems[part, i] = value[i * HALF : (i + 1) * HALF]
        rems[part, 2] = last[part * HALF : (part + 1) * HALF]

    down = ((1,), (0,))
    shift = HALF - rest
    sends = []

    def send(level, lanes):
        copy = pltpu.make_async_copy(out.at[level, :, lanes], final.at[level, :, lanes], sent_sems.at[len(sends)])
        copy.start()
        sends.append(copy)

    for level in range(levels):
        which = (odd, 1 - odd, 2)[level]
        for part in range(2):
            value = get_rows(got, level * STEP + part * 8, groups).T
            for base, piece in zip((0, size), split(value)):
                zs[level, part, base : base + LANES] = piece
            for base, piece in zip((0, size), split(rems[part, which])):
                zs[level, part, base + LANES : base + size] = piece
        if level == 0:
            for fetch in fetches[1:5]:
                fetch.wait()
        if more:
            fetches[5 + level].wait()

        def store(lanes, value):
            full, tail = value[:LANES], value[LANES:]
            tail = jnp.where(upper == 1, tail[shift:], tail[:rest])
            for start, piece in ((rest * upper, full), (LANES * (1 - upper), tail)):
                where = at(start, piece.shape[0], 8)
                out[level, where, lanes] = piece + out[level, where, lanes] if more else piece

        for tile in range(half // TILE):
            where = slice(tile * TILE, (tile + 1) * TILE)
            sums = []
            for part in range(2):
                high, low = tables[2 * part], tables[2 * part + 1]
                both = dot(zs[level, part], high[:, where], down)
                sums.append(both[:size] + (both[size:] + dot(zs[level, part, :size], low[:, where], down)))
            store(where, sums[0] + sums[1])
            other = sums[0] - sums[1]
            for piece in range(TILE // LANES):
                start = 2 * half - tile * TILE - (piece + 1) * LANES
                end = min(start + LANES, cols)
                store(slice(start, end), mirror(other[:, piece * LANES : (piece + 1) * LANES])[:, : end - start])
            if level == levels - 1:
                send(level, pl.ds(tile * TILE, TILE))
                start = 2 * half - (tile + 1) * TILE
                send(level, pl.ds(start, min(start + TILE, cols) - start))
        if level < levels - 1:
            send(level, pl.ds(0, cols))
    for copy in sends:
        copy.wait()


def packs(wide, lev, levels, rows, cols):
    share = 2 * KT // (wide * lev)
    return (
        levels == 3
        and wide % 8 == 0
        and LANES < rows <= LANES + HALF
        and rows % 8 == 0
        and (LANES + HALF - rows) * wide == E
        and cols % LANES == HALF == E
        and (cols + E) % (2 * TILE) == 0
        and (wide * lev * 8) % TILE == 0
        and share % STEP == 0
        and (STEP + STEP // 2) * (LANES + HALF - rows) % HALF == 0
        and (rows - LANES) % (LANES + HALF - rows) == 0
        and KT // 8 <= LANES
    )


def wave_seeds(doubled, length):
    turn = np.pi / length
    seeds = []
    for waves in (np.arange(0, KT, STEP), np.arange(STEP)):
        angle = turn * ((waves[:, None] * doubled[None, :]) % (2 * length))
        seeds += [np.cos(angle), np.sin(angle)]
    return [np.asarray(a, np.float32) for a in seeds]


def packed(state, to_modes, from_modes, mode_depth):
    wide, lev = lax.axis_size("wide"), lax.axis_size("lev")
    levels, rows, cols = state.shape
    devices = wide * lev
    length = cols + E
    half = length // 2
    chunks = 2 * KT // (devices * STEP)
    width = devices * 8
    tail = rows - LANES
    extra = E // wide
    block = levels * STEP + dense_rows(tail)[0]
    total = lev * levels
    f32, bf16 = jnp.float32, jnp.bfloat16

    starts = np.arange(wide // 2)[:, None]
    order = np.concatenate(
        [
            (starts * rows + np.arange(LANES)).reshape(-1),
            np.concatenate(
                [starts * rows + LANES + np.arange(tail), cols + starts * extra + np.arange(extra)], axis=1
            ).reshape(-1),
        ]
    )
    seeds_x = wave_seeds(2 * np.arange(half) + 1, length)
    seeds_y = wave_seeds(2 * order - (cols - 1), length)
    weights = edge_weights(E)
    edge_x = np.concatenate([np.zeros((4, HALF), np.float32), weights], axis=1)
    edge_y = np.zeros((2, 4, half), np.float32)
    outside = order >= cols
    ahead, behind = weights[:, order[outside] - cols], weights[:, E - 1 - (order[outside] - cols)]
    edge_y[0][:, outside], edge_y[1][:, outside] = ahead + behind, ahead - behind
    edge_y = edge_y[:, :, wide // 2 * LANES :]
    waves = np.arange(KT)
    lap = 4.0 * np.sin(np.pi * waves / length) ** 2
    facts = np.stack([lap, waves * waves, np.where(waves == 0, 1.0, 2.0)]).astype(np.float32)
    own = np.zeros((3, STEP, LANES), np.float32)
    own[:, :, : KT // 8] = np.tile(facts.reshape(3, -1, 8).transpose(0, 2, 1), (1, 2, 1))
    line = np.tile(facts, (1, 2))
    line[2] /= length * length

    wide_index = lax.axis_index("wide")
    place = jnp.stack([lax.rem(wide_index, 2), (wide_index >= wide // 2).astype(jnp.int32)])
    me = (wide_index * lev + lax.axis_index("lev")).reshape(1)
    smem = pl.BlockSpec(memory_space=pltpu.SMEM)
    vmem = pl.BlockSpec(memory_space=pltpu.VMEM)
    anywhere = pl.BlockSpec(memory_space=pl.ANY)
    table = (KT, half)

    def params(mib):
        return pltpu.CompilerParams(vmem_limit_bytes=mib << 20)

    def whole(a):
        return pl.BlockSpec(a.shape, lambda i: (0,) * a.ndim)

    def cost(flops, size):
        return pl.CostEstimate(flops=flops, bytes_accessed=size, transcendentals=0)

    def hbm(a):
        return pltpu.with_memory_space_constraint(a, pltpu.HBM)

    def to_columns(chunk):
        operands = [hbm(jnp.asarray(a)) for a in (edge_x, *seeds_x)]
        size = LANES + HALF
        return pl.pallas_call(
            functools.partial(forward_x, chunk),
            in_specs=[smem] + [anywhere] * (1 + len(operands)),
            out_specs=vmem,
            out_shape=jax.ShapeDtypeStruct((devices * block, LANES), f32),
            scratch_shapes=[
                *[pltpu.VMEM((width, half), bf16)] * 4,
                *[pltpu.VMEM((levels, 2 * size, half), bf16)] * 2,
                pltpu.VMEM(state.shape, f32),
                pltpu.VMEM((devices * (STEP + STEP // 2), LANES), f32),
                *[pltpu.VMEM(a.shape, f32) for a in operands],
                pltpu.SemaphoreType.DMA((levels,)),
                pltpu.SemaphoreType.DMA((len(operands),)),
            ],
            compiler_params=params(LIMITS[0]),
            cost_estimate=cost(12 * width * levels * size * half, 8 << 20),
            name=f"forward_x_{chunk}",
        )(place, hbm(state), *operands)

    def all_tables(after):
        operands = [hbm(jnp.asarray(a)) for a in (*seeds_x, *seeds_y)]
        steps = KT // TILE
        return pl.pallas_call(
            make_tables,
            grid=(steps,),
            in_specs=[anywhere] + [whole(a) for a in operands],
            out_specs=[pl.BlockSpec((TILE, half), lambda i: (i, 0))] * 4
            + [pl.BlockSpec((2, TILE, half), lambda i: (0, i, 0))] * 2,
            out_shape=[pltpu.HBM(table, bf16)] * 4 + [pltpu.HBM((2, *table), bf16)] * 2,
            compiler_params=params(LIMITS[1]),
            cost_estimate=cost(32 * KT * half, 8 << 20),
            name="make_tables",
        )(after, *operands)

    def through(chunk, got, high, low):
        operands = [got, hbm(high), hbm(low), *(jnp.asarray(a) for a in (edge_y, own, line))]
        span = total * STEP
        return pl.pallas_call(
            functools.partial(middle, chunk, devices, wide=wide, tail=tail),
            in_specs=[smem] * 4 + [vmem] * len(operands),
            out_specs=vmem,
            out_shape=jax.ShapeDtypeStruct(got.shape, f32),
            scratch_shapes=[
                pltpu.VMEM((2, 2 * span, half), bf16),
                pltpu.VMEM((2 * span, 2 * KT), bf16),
                pltpu.VMEM((span, LANES), f32),
                *[pltpu.VMEM((devices, (levels + 1) * STEP + STEP // 2, LANES), f32)] * 2,
            ],
            compiler_params=params(LIMITS[2]),
            cost_estimate=cost(24 * span * KT * half, 6 << 20),
            name=f"middle_{chunk}",
        )(me, to_modes, from_modes, mode_depth, *operands)

    def to_rows(chunk, got, tables, prior):
        size = LANES + HALF
        more = prior is not None
        return pl.pallas_call(
            functools.partial(inverse_x, chunk, more=more),
            in_specs=[smem] + [anywhere] * (5 + more),
            out_specs=anywhere,
            out_shape=jax.ShapeDtypeStruct(state.shape, f32) if more else pltpu.HBM(state.shape, f32),
            scratch_shapes=[
                pltpu.VMEM(got.shape, f32),
                pltpu.VMEM(state.shape, f32),
                pltpu.VMEM((levels, 2, 2 * size, width), bf16),
                pltpu.VMEM((2, levels, HALF, width), f32),
                *[pltpu.VMEM((width, half), bf16)] * 4,
                pltpu.VMEM((devices * (STEP + STEP // 2), LANES), f32),
                pltpu.SemaphoreType.DMA((5 + levels,)),
                pltpu.SemaphoreType.DMA((levels - 1 + 2 * (half // TILE),)),
            ],
            compiler_params=params(LIMITS[3]),
            cost_estimate=cost(12 * width * levels * size * half, 8 << 20),
            name=f"inverse_x_{chunk}",
        )(place, got, *map(hbm, tables), *([hbm(prior)] if more else []))

    def exchange(sent):
        return lax.all_to_all(sent.reshape(-1, 1, LANES), AXES, 0, 0, tiled=True).reshape(sent.shape)

    sent = [to_columns(chunk) for chunk in range(chunks)]
    tables = all_tables(sent[-1])
    high, low = (a.reshape(2 * KT, half) for a in tables[4:])
    arrived = [exchange(part) for part in sent]
    returned = [exchange(through(chunk, got, high, low)) for chunk, got in enumerate(arrived)]
    value = None
    for chunk, got in enumerate(returned):
        value = to_rows(chunk, got, tables[:4], value)
    return value


def solution(mesh):
    placed = (P("lev", "wide", None), P(), P(), P())

    def shards(state, *rest):
        fits = packs(lax.axis_size("wide"), lax.axis_size("lev"), *state.shape)
        return (packed if fits else plain)(state, *rest)

    return jax.shard_map(
        shards, mesh=mesh, in_specs=placed, out_specs=P("lev", "wide", None), check_vma=False
    )
```

```python
import functools

import jax
import jax.numpy as jnp
import numpy as np
from jax import lax
from jax.experimental import pallas as pl
from jax.experimental.pallas import tpu as pltpu
from jax.sharding import PartitionSpec as P

I = 1472
E = 64
KT = 512
STEP = 16
LANES = 128
HALF = 64
TILE = 256

HIGH = lax.Precision.HIGH
HIGHEST = lax.Precision.HIGHEST
AXES = ("wide", "lev")


def blend_weights(extra):
    f = (np.arange(extra, dtype=np.float64) + 1.0) / (extra + 1.0)
    f2, f3 = f * f, f * f * f
    return 2 * f3 - 3 * f2 + 1, f3 - 2 * f2 + f, -2 * f3 + 3 * f2, f3 - f2


def edge_weights(extra):
    h00, h10, h01, h11 = blend_weights(extra)
    return np.stack([h01 - h11, h11, -h10, h00 + h10]).astype(np.float32)


def extend(block, extra):
    w = jnp.asarray(edge_weights(extra))
    added = (
        block[..., :1] * w[0] + block[..., 1:2] * w[1] + block[..., -2:-1] * w[2] + block[..., -1:] * w[3]
    )
    return jnp.concatenate([block, added], axis=-1)


def cas_seeds(waves, positions, length):
    turn = 2.0 * np.pi / length
    base = waves[::STEP].astype(np.int64)
    coarse = turn * ((base[:, None] * positions[None, :]) % length)
    fine = turn * ((np.arange(STEP)[:, None] * positions[None, :]) % length)
    parts = np.cos(coarse) + np.sin(coarse), np.cos(coarse) - np.sin(coarse), np.cos(fine), np.sin(fine)
    return [np.asarray(a, np.float32) for a in parts]


def cas_table(waves, positions, length):
    plus, minus, cosine, sine = (jnp.asarray(a) for a in cas_seeds(waves, positions, length))
    table = plus[:, None, :] * cosine[None] + minus[:, None, :] * sine[None]
    return table.reshape(len(waves), len(positions))


def plain(state, to_modes, from_modes, mode_depth):
    wide, lev = lax.axis_size("wide"), lax.axis_size("lev")
    devices = wide * lev
    levels, rows, cols = state.shape
    length = I + E
    waves = np.arange(-KT, KT)
    share = len(waves) // devices
    table = cas_table(waves, np.arange(length), length)
    spec = jnp.einsum("qn,lrn->qlr", table, extend(state, E), precision=HIGH)
    spec = spec.reshape(devices, share, levels * rows)
    spec = lax.all_to_all(spec, AXES, 0, 0, tiled=True)
    spec = spec.reshape(wide, lev, share, levels, rows).transpose(1, 3, 2, 0, 4)
    spec = extend(spec.reshape(lev * levels, share, wide * rows), E)
    spec = jnp.einsum("lqr,pr->lqp", spec, table, precision=HIGH)
    first = (lax.axis_index("wide") * lev + lax.axis_index("lev")) * share
    lap = (4.0 * np.sin(np.pi * waves / length) ** 2).astype(np.float32)
    square = (waves * waves).astype(np.int32)
    lap_q = lax.dynamic_slice_in_dim(jnp.asarray(lap), first, share)
    square_q = lax.dynamic_slice_in_dim(jnp.asarray(square), first, share)
    keep = (square_q[:, None] + square[None, :] < KT * KT).astype(jnp.float32)
    modes = jnp.einsum("ml,lqp->mqp", to_modes, spec, precision=HIGHEST)
    solved = modes * keep / (1.0 + mode_depth[:, None, None] * (lap_q[:, None] + lap[None, :]))
    mixed = jnp.einsum("lm,mqp->lqp", from_modes, solved, precision=HIGHEST)
    back = jnp.einsum("lqp,pr->lqr", mixed, table[:, :I], precision=HIGH)
    back = back.reshape(lev, levels, share, wide, rows).transpose(3, 0, 2, 1, 4)
    back = lax.all_to_all(back.reshape(devices, share, levels * rows), AXES, 0, 0, tiled=True)
    back = back.reshape(len(waves), levels, rows)
    return jnp.einsum("qlr,qn->lrn", back, table[:, :I], precision=HIGH) / (length * length)


LIMITS = (16, 16, 20, 16)


def split(value):
    high = value.astype(jnp.bfloat16)
    return high, (value - high.astype(jnp.float32)).astype(jnp.bfloat16)


def dot(a, b, contract):
    return lax.dot_general(a, b, (contract, ((), ())), preferred_element_type=jnp.float32)


def left_half():
    return lax.broadcasted_iota(jnp.int32, (1, LANES), 1) < HALF


def swap(value):
    return pltpu.roll(value, HALF, 1)


def mirror(value):
    order = LANES - 1 - lax.broadcasted_iota(jnp.int32, value.shape, 1)
    return jnp.take_along_axis(value, order, axis=1)


def put_rows(ref, start, value):
    height = ref.shape[0] * 8 // value.shape[0]
    for d in range(value.shape[0] // 8):
        ref[d * height + start : d * height + start + 8] = value[d * 8 : d * 8 + 8]


def get_rows(ref, start, count):
    height = ref.shape[0] // count
    return jnp.concatenate([ref[pl.ds(start + d * height, 8)] for d in range(count)], axis=0)


def strided(ref, start, count):
    height = ref.shape[0] // count

    def read(j):
        return ref[pl.ds(start + j, count, stride=height)]

    def write(j, value):
        ref[pl.ds(start + j, count, stride=height)] = value

    return read, write


def empty_lanes(upper, rest):
    lane = lax.broadcasted_iota(jnp.int32, (1, LANES), 1) + rest * upper
    return lax.rem(lane, HALF) >= rest


def dense_rows(rest):
    lasting = STEP + STEP // 2
    return lasting - lasting * (HALF - rest) // HALF, HALF - rest


def fold_rows(read, write, empty, rest):
    kept, gap = dense_rows(rest)
    each = rest // gap
    for j in range(kept):
        moved = pltpu.roll(read(kept + j // each), rest - gap * (j % each), 1)
        write(j, jnp.where(empty, moved, read(j)))


def unfold_rows(read, write, empty, rest):
    kept, gap = dense_rows(rest)
    each = rest // gap
    for i in range(kept // each):
        back = 0.0
        for j in range(i * each, (i + 1) * each):
            value = read(j)
            write(j, jnp.where(empty, 0.0, value))
            back = back + pltpu.roll(jnp.where(empty, value, 0.0), LANES - rest + gap * (j % each), 1)
        write(kept + i, back)


def at(start, size, unit):
    return pl.ds(start if isinstance(start, int) else pl.multiple_of(start, unit), size)


def fill_tables(seeds, first, cos_high, cos_low, sin_high, sin_low):
    coarse_cos, coarse_sin, fine_cos, fine_sin = seeds
    for lane in range(0, cos_high.shape[-1], TILE):
        lanes = slice(lane, lane + TILE)
        fine_c, fine_s = fine_cos[:, lanes], fine_sin[:, lanes]
        for group in range(cos_high.shape[0] // STEP):
            rows = slice(group * STEP, (group + 1) * STEP)
            pick = pl.ds(first + group, 1)
            coarse_c, coarse_s = coarse_cos[pick, lanes], coarse_sin[pick, lanes]
            cos_high[rows, lanes], cos_low[rows, lanes] = split(coarse_c * fine_c - coarse_s * fine_s)
            sin_high[rows, lanes], sin_low[rows, lanes] = split(coarse_s * fine_c + coarse_c * fine_s)


def make_tables(order, *refs):
    seeds_x, seeds_y, tables_x, (high, low) = refs[:4], refs[4:8], refs[8:12], refs[12:]
    first = pl.program_id(0) * (tables_x[0].shape[0] // STEP)
    fill_tables(seeds_x, first, *tables_x)
    fill_tables(seeds_y, first, high.at[0], low.at[0], high.at[1], low.at[1])


def forward_x(chunk, place, x, edge_in, *refs):
    sources, (out, *tables, even, uneven, buffer, packed), rest_refs = refs[:4], refs[4:13], refs[13:]
    edge, *seeds, in_sems, seed_sems = rest_refs
    levels, rows, cols = x.shape
    waves = tables[0].shape[0]
    groups = waves // 8
    size = LANES + HALF
    half = tables[0].shape[1]
    odd, upper = place[0], place[1]
    rest = rows - LANES
    block = 32

    def fetch(level):
        return pltpu.make_async_copy(x.at[level], buffer.at[level], in_sems.at[level])

    smalls = [
        pltpu.make_async_copy(source, target, seed_sems.at[i])
        for i, (source, target) in enumerate(zip((*sources, edge_in), (*seeds, edge)))
    ]
    for small in smalls:
        small.start()
    for level in range(levels):
        fetch(level).start()
    for small in smalls:
        small.wait()
    fill_tables(seeds, chunk * (waves // STEP), *tables)

    def reflect(level):
        fetch(level).wait()
        for r in range(0, size, block):

            def read(lanes):
                if r < LANES:
                    return buffer[level, at(rest * upper + r, block, 8), lanes]
                first = r - LANES
                live = min(block, rest - first)
                low = buffer[level, LANES + first : LANES + first + live, lanes]
                if live < block:
                    low = jnp.concatenate([low, jnp.zeros((block - live, low.shape[1]), low.dtype)], axis=0)
                shift = HALF - rest
                if first < shift:
                    high = buffer[level, 0 : block - shift, lanes]
                    high = jnp.concatenate([jnp.zeros((shift, high.shape[1]), high.dtype), high], axis=0)
                else:
                    high = buffer[level, first - shift : first - shift + block, lanes]
                return jnp.where(upper == 1, high, low)

            where = slice(r, r + block)
            above = slice(size + r, size + r + block)
            for tile in range(half // LANES):
                lanes = slice(tile * LANES, (tile + 1) * LANES)
                value = read(lanes)
                start = cols + HALF - (tile + 1) * LANES
                other = read(slice(start, min(start + LANES, cols)))
                if tile == 0:
                    ends = (value[:, 0:1], value[:, 1:2], other[:, HALF - 2 : HALF - 1], other[:, HALF - 1 : HALF])
                    other = jnp.concatenate([other, jnp.zeros_like(other)], axis=1)
                    for i, end in enumerate(ends):
                        other = other + end * edge[i : i + 1]
                other = mirror(other)
                even[level, where, lanes], even[level, above, lanes] = split(value + other)
                uneven[level, where, lanes], uneven[level, above, lanes] = split(value - other)

    def transform(level):
        across = ((1,), (1,))
        blank = jnp.zeros((HALF, waves), jnp.float32)
        for part, (source, high, low) in enumerate(((even, *tables[:2]), (uneven, *tables[2:]))):
            both = dot(source[level], high[...], across)
            spec = both[:size] + (both[size:] + dot(source[level, :size], low[...], across))
            full = spec[:LANES].T
            first = level * STEP + part * 8
            put_rows(out, first, full)
            if level < 2:
                first = part * 8
                if level == 0:
                    put_rows(packed, first, jnp.concatenate([spec[LANES:], blank], axis=0).T)
                else:
                    turned = jnp.concatenate([blank, spec[LANES:]], axis=0).T
                    value = get_rows(packed, first, groups) + turned
                    put_rows(packed, first, jnp.where(odd == 1, swap(value), value))
            elif part == 0:
                cosines = spec[LANES:]
            else:
                put_rows(packed, STEP, jnp.concatenate([cosines, spec[LANES:]], axis=0).T)

    reflect(0)
    for level in range(levels):
        if level + 1 < levels:
            reflect(level + 1)
        transform(level)
    fold_rows(
        strided(packed, 0, groups)[0], strided(out, levels * STEP, groups)[1], empty_lanes(upper, rest), rest
    )


def middle(
    chunk, devices, me, to_modes, from_modes, depth, arrived, *refs, wide, tail
):
    high, low, edge, own, line, leaving, xs, ms, ends, got, out = refs
    count = got.shape[0]
    lev = count // wide
    total = to_modes.shape[0]
    levels = total // lev
    span = total * STEP
    pairs = wide // 2
    left = left_half()
    rem = slice(levels * STEP, (levels + 1) * STEP)
    rem2 = slice((levels + 1) * STEP, (levels + 1) * STEP + STEP // 2)
    half = high.shape[1]
    waves = high.shape[0] // 2

    def rows_of(lv, level):
        start = (lv * levels + level) * STEP
        return start, slice(start, start + STEP)

    height = arrived.shape[0] // count
    block_index = lax.broadcasted_iota(jnp.int32, (count, 1), 0)
    empty = empty_lanes((block_index >= count // 2).astype(jnp.int32), tail)
    fulls = levels * STEP
    for d in range(count):
        got[d, :fulls] = arrived[d * height : d * height + fulls]

    def keep_row(j, value):
        got[:, fulls + j] = value

    def send_row(j, value):
        leaving[pl.ds(fulls + j, count, stride=height)] = value

    unfold_rows(lambda j: arrived[pl.ds(fulls + j, count, stride=height)], keep_row, empty, tail)

    for lv in range(lev):
        for level in range(levels):
            rows = rows_of(lv, level)[1]
            full = slice(level * STEP, (level + 1) * STEP)
            ends[rows, 0:2] = got[lv, full, 0:2]
            ends[rows, 2:4] = got[(wide - 1) * lev + lv, full, LANES - 2 : LANES]

    def put(part, start, lanes, value):
        for base, piece in zip((0, span), split(value)):
            xs[part, base + start : base + start + value.shape[0], lanes] = piece

    def gather(pair, carry):
        weights = edge[:, :, at(pair * LANES, LANES, LANES)]
        for lv in range(lev):
            a, b = 2 * pair, 2 * pair + 1
            low_a, low_b = a * lev + lv, b * lev + lv
            top_a, top_b = (wide - 1 - a) * lev + lv, (wide - 1 - b) * lev + lv
            for level in range(levels):
                start = rows_of(lv, level)[0]
                full = slice(level * STEP, (level + 1) * STEP)
                for w, src, top in ((a, low_a, top_a), (b, low_b, top_b)):
                    value, other = got[src, full], mirror(got[top, full])
                    lanes = at(w * LANES, LANES, LANES)
                    put(0, start, lanes, value + other)
                    put(1, start, lanes, value - other)
            turned = mirror(got[top_a, rem]), mirror(got[top_b, rem])
            turned2 = swap(mirror(got[top_a, rem2])), swap(mirror(got[top_b, rem2]))
            for part, sign in ((0, 1.0), (1, -1.0)):
                fa, fb = got[low_a, rem] + sign * turned[0], got[low_b, rem] + sign * turned[1]
                ga, gb = got[low_a, rem2] + sign * turned2[0], got[low_b, rem2] + sign * turned2[1]
                values = (
                    jnp.where(left, fa, fb),
                    swap(jnp.where(left, fb, fa)),
                    jnp.concatenate([jnp.where(left, ga, swap(gb)), jnp.where(left, swap(ga), gb)], axis=0),
                )
                for level, value in enumerate(values):
                    start, rows = rows_of(lv, level)
                    for i in range(4):
                        value = value + ends[rows, i : i + 1] * weights[part, i : i + 1]
                    put(part, start, at(pairs * LANES + pair * LANES, LANES, LANES), value)
        return carry

    lax.fori_loop(0, pairs // 2, gather, 0)

    group = chunk * devices + me[0]
    mine = lax.broadcasted_iota(jnp.int32, (1, LANES), 1) == group
    lap_q, square_q, weight_q = (
        jnp.sum(jnp.where(mine, own[i], 0.0), axis=1, keepdims=True) for i in range(3)
    )

    def solve(tile, carry):
        where = at(tile * TILE, TILE, TILE)
        part = tile // (waves // TILE)
        across = ((1,), (1,))
        both = dot(xs[part], high[where], across)
        spec = both[:span] + (both[span:] + dot(xs[part, :span], low[where], across))
        for piece in range(TILE // LANES):
            lanes = slice(piece * LANES, (piece + 1) * LANES)
            here = at(tile * TILE + piece * LANES, LANES, LANES)
            lap = lap_q + line[0:1, here]
            scale = jnp.where(square_q + line[1:2, here] < float(KT * KT), weight_q * line[2:3, here], 0.0)
            parts = [spec[l * STEP : (l + 1) * STEP, lanes] for l in range(total)]
            solved = []
            for m in range(total):
                mode = sum(to_modes[m, l] * parts[l] for l in range(total))
                solved.append(mode * scale / (1.0 + depth[m] * lap))
            for l in range(total):
                mixed = sum(from_modes[l, m] * solved[m] for m in range(total))
                for base, value in zip((0, span), split(mixed)):
                    ms[base + l * STEP : base + (l + 1) * STEP, here] = value
        return carry

    lax.fori_loop(0, 2 * waves // TILE, solve, 0)

    def back(start):
        where = at(start, TILE, TILE)
        down = ((1,), (0,))
        sums = []
        for part in range(2):
            k = slice(part * waves, (part + 1) * waves)
            both = dot(ms[:, k], high[k, where], down)
            sums.append(both[:span] + (both[span:] + dot(ms[:span, k], low[k, where], down)))
        return sums[0] + sums[1], sums[0] - sums[1]

    def scatter(pair, carry):
        values = back(pair * TILE)
        for piece in range(2):
            w = 2 * pair + piece
            lanes = slice(piece * LANES, (piece + 1) * LANES)
            for lv in range(lev):
                for level in range(levels):
                    rows = rows_of(lv, level)[1]
                    full = slice(level * STEP, (level + 1) * STEP)
                    out[w * lev + lv, full] = values[0][rows, lanes]
                    out[(wide - 1 - w) * lev + lv, full] = mirror(values[1][rows, lanes])
        return carry

    lax.fori_loop(0, pairs // 2, scatter, 0)

    for quad in range(pairs // 4):
        values = back(pairs * LANES + quad * TILE)
        for piece in range(2):
            pair = 2 * quad + piece
            lanes = slice(piece * LANES, (piece + 1) * LANES)
            for lv in range(lev):
                packs_of = []
                for value in values:
                    zero, one, two = (value[rows_of(lv, level)[1], lanes] for level in range(3))
                    one = swap(one)
                    cos, sin = two[: STEP // 2], two[STEP // 2 :]
                    packs_of.append(
                        (
                            (jnp.where(left, zero, one), jnp.where(left, cos, swap(sin))),
                            (jnp.where(left, one, zero), jnp.where(left, swap(cos), sin)),
                        )
                    )
                for i in range(2):
                    w = 2 * pair + i
                    out[w * lev + lv, rem], out[w * lev + lv, rem2] = packs_of[0][i]
                    top = (wide - 1 - w) * lev + lv
                    out[top, rem], out[top, rem2] = mirror(packs_of[1][i][0]), swap(mirror(packs_of[1][i][1]))

    for d in range(count):
        leaving[d * height : d * height + fulls] = out[d, :fulls]
    fold_rows(lambda j: out[:, fulls + j], send_row, empty, tail)


def inverse_x(chunk, place, got, *refs, more):
    sources, refs = refs[:4], refs[4:]
    prior, refs = (refs[0], refs[1:]) if more else (None, refs)
    final, out, zs, rems, *tables, unpacked, sems, sent_sems = refs
    levels, rows, cols = out.shape
    waves, half = tables[0].shape
    size = LANES + HALF
    odd, upper = place[0], place[1]
    rest = rows - LANES
    groups = waves // 8

    copies = [(source.at[pl.ds(chunk * waves, waves)], target) for source, target in zip(sources, tables)]
    copies += [(prior.at[level], out.at[level]) for level in range(levels)] if more else []
    fetches = [pltpu.make_async_copy(*pair, sems.at[i]) for i, pair in enumerate(copies)]
    for fetch in fetches:
        fetch.start()

    unfold_rows(
        strided(got, levels * STEP, groups)[0], strided(unpacked, 0, groups)[1], empty_lanes(upper, rest), rest
    )
    last = get_rows(unpacked, STEP, groups).T
    for part in range(2):
        value = get_rows(unpacked, part * 8, groups).T
        for i in range(2):
            rems[part, i] = value[i * HALF : (i + 1) * HALF]
        rems[part, 2] = last[part * HALF : (part + 1) * HALF]

    down = ((1,), (0,))
    shift = HALF - rest
    sends = []

    def send(level, lanes):
        copy = pltpu.make_async_copy(out.at[level, :, lanes], final.at[level, :, lanes], sent_sems.at[len(sends)])
        copy.start()
        sends.append(copy)

    for level in range(levels):
        which = (odd, 1 - odd, 2)[level]
        for part in range(2):
            value = get_rows(got, level * STEP + part * 8, groups).T
            for base, piece in zip((0, size), split(value)):
                zs[level, part, base : base + LANES] = piece
            for base, piece in zip((0, size), split(rems[part, which])):
                zs[level, part, base + LANES : base + size] = piece
        if level == 0:
            for fetch in fetches[:4]:
                fetch.wait()
        if more:
            fetches[4 + level].wait()

        def store(lanes, value):
            full, tail = value[:LANES], value[LANES:]
            tail = jnp.where(upper == 1, tail[shift:], tail[:rest])
            for start, piece in ((rest * upper, full), (LANES * (1 - upper), tail)):
                where = at(start, piece.shape[0], 8)
                out[level, where, lanes] = piece + out[level, where, lanes] if more else piece

        for tile in range(half // TILE):
            where = slice(tile * TILE, (tile + 1) * TILE)
            sums = []
            for part in range(2):
                high, low = tables[2 * part], tables[2 * part + 1]
                both = dot(zs[level, part], high[:, where], down)
                sums.append(both[:size] + (both[size:] + dot(zs[level, part, :size], low[:, where], down)))
            store(where, sums[0] + sums[1])
            other = sums[0] - sums[1]
            for piece in range(TILE // LANES):
                start = 2 * half - tile * TILE - (piece + 1) * LANES
                end = min(start + LANES, cols)
                store(slice(start, end), mirror(other[:, piece * LANES : (piece + 1) * LANES])[:, : end - start])
            if level == levels - 1:
                send(level, pl.ds(tile * TILE, TILE))
                start = 2 * half - (tile + 1) * TILE
                send(level, pl.ds(start, min(start + TILE, cols) - start))
        if level < levels - 1:
            send(level, pl.ds(0, cols))
    for copy in sends:
        copy.wait()


def packs(wide, lev, levels, rows, cols):
    share = 2 * KT // (wide * lev)
    return (
        levels == 3
        and wide % 8 == 0
        and LANES < rows <= LANES + HALF
        and rows % 8 == 0
        and (LANES + HALF - rows) * wide == E
        and cols % LANES == HALF == E
        and (cols + E) % (2 * TILE) == 0
        and (wide * lev * 8) % TILE == 0
        and share % STEP == 0
        and (STEP + STEP // 2) * (LANES + HALF - rows) % HALF == 0
        and (rows - LANES) % (LANES + HALF - rows) == 0
        and KT // 8 <= LANES
    )


def wave_seeds(doubled, length):
    turn = np.pi / length
    seeds = []
    for waves in (np.arange(0, KT, STEP), np.arange(STEP)):
        angle = turn * ((waves[:, None] * doubled[None, :]) % (2 * length))
        seeds += [np.cos(angle), np.sin(angle)]
    return [np.asarray(a, np.float32) for a in seeds]


def packed(state, to_modes, from_modes, mode_depth):
    wide, lev = lax.axis_size("wide"), lax.axis_size("lev")
    levels, rows, cols = state.shape
    devices = wide * lev
    length = cols + E
    half = length // 2
    chunks = 2 * KT // (devices * STEP)
    width = devices * 8
    tail = rows - LANES
    extra = E // wide
    block = levels * STEP + dense_rows(tail)[0]
    total = lev * levels
    f32, bf16 = jnp.float32, jnp.bfloat16

    starts = np.arange(wide // 2)[:, None]
    order = np.concatenate(
        [
            (starts * rows + np.arange(LANES)).reshape(-1),
            np.concatenate(
                [starts * rows + LANES + np.arange(tail), cols + starts * extra + np.arange(extra)], axis=1
            ).reshape(-1),
        ]
    )
    seeds_x = wave_seeds(2 * np.arange(half) + 1, length)
    seeds_y = wave_seeds(2 * order - (cols - 1), length)
    weights = edge_weights(E)
    edge_x = np.concatenate([np.zeros((4, HALF), np.float32), weights], axis=1)
    edge_y = np.zeros((2, 4, half), np.float32)
    outside = order >= cols
    ahead, behind = weights[:, order[outside] - cols], weights[:, E - 1 - (order[outside] - cols)]
    edge_y[0][:, outside], edge_y[1][:, outside] = ahead + behind, ahead - behind
    edge_y = edge_y[:, :, wide // 2 * LANES :]
    waves = np.arange(KT)
    lap = 4.0 * np.sin(np.pi * waves / length) ** 2
    facts = np.stack([lap, waves * waves, np.where(waves == 0, 1.0, 2.0)]).astype(np.float32)
    own = np.zeros((3, STEP, LANES), np.float32)
    own[:, :, : KT // 8] = np.tile(facts.reshape(3, -1, 8).transpose(0, 2, 1), (1, 2, 1))
    line = np.tile(facts, (1, 2))
    line[2] /= length * length

    wide_index = lax.axis_index("wide")
    place = jnp.stack([lax.rem(wide_index, 2), (wide_index >= wide // 2).astype(jnp.int32)])
    me = (wide_index * lev + lax.axis_index("lev")).reshape(1)
    smem = pl.BlockSpec(memory_space=pltpu.SMEM)
    vmem = pl.BlockSpec(memory_space=pltpu.VMEM)
    anywhere = pl.BlockSpec(memory_space=pl.ANY)
    table = (KT, half)

    def params(mib):
        return pltpu.CompilerParams(vmem_limit_bytes=mib << 20)

    def whole(a):
        return pl.BlockSpec(a.shape, lambda i: (0,) * a.ndim)

    def cost(flops, size):
        return pl.CostEstimate(flops=flops, bytes_accessed=size, transcendentals=0)

    def hbm(a):
        return pltpu.with_memory_space_constraint(a, pltpu.HBM)

    def to_columns(chunk):
        operands = [hbm(jnp.asarray(a)) for a in (edge_x, *seeds_x)]
        size = LANES + HALF
        return pl.pallas_call(
            functools.partial(forward_x, chunk),
            in_specs=[smem] + [anywhere] * (1 + len(operands)),
            out_specs=vmem,
            out_shape=jax.ShapeDtypeStruct((devices * block, LANES), f32),
            scratch_shapes=[
                *[pltpu.VMEM((width, half), bf16)] * 4,
                *[pltpu.VMEM((levels, 2 * size, half), bf16)] * 2,
                pltpu.VMEM(state.shape, f32),
                pltpu.VMEM((devices * (STEP + STEP // 2), LANES), f32),
                *[pltpu.VMEM(a.shape, f32) for a in operands],
                pltpu.SemaphoreType.DMA((levels,)),
                pltpu.SemaphoreType.DMA((len(operands),)),
            ],
            compiler_params=params(LIMITS[0]),
            cost_estimate=cost(12 * width * levels * size * half, 8 << 20),
            name=f"forward_x_{chunk}",
        )(place, hbm(state), *operands)

    def all_tables(after):
        operands = [hbm(jnp.asarray(a)) for a in (*seeds_x, *seeds_y)]
        steps = KT // TILE
        return pl.pallas_call(
            make_tables,
            grid=(steps,),
            in_specs=[anywhere] + [whole(a) for a in operands],
            out_specs=[pl.BlockSpec((TILE, half), lambda i: (i, 0))] * 4
            + [pl.BlockSpec((2, TILE, half), lambda i: (0, i, 0))] * 2,
            out_shape=[pltpu.HBM(table, bf16)] * 4 + [pltpu.HBM((2, *table), bf16)] * 2,
            compiler_params=params(LIMITS[1]),
            cost_estimate=cost(32 * KT * half, 8 << 20),
            name="make_tables",
        )(after, *operands)

    def through(chunk, got, high, low):
        operands = [got, hbm(high), hbm(low), *(jnp.asarray(a) for a in (edge_y, own, line))]
        span = total * STEP
        return pl.pallas_call(
            functools.partial(middle, chunk, devices, wide=wide, tail=tail),
            in_specs=[smem] * 4 + [vmem] * len(operands),
            out_specs=vmem,
            out_shape=jax.ShapeDtypeStruct(got.shape, f32),
            scratch_shapes=[
                pltpu.VMEM((2, 2 * span, half), bf16),
                pltpu.VMEM((2 * span, 2 * KT), bf16),
                pltpu.VMEM((span, LANES), f32),
                *[pltpu.VMEM((devices, (levels + 1) * STEP + STEP // 2, LANES), f32)] * 2,
            ],
            compiler_params=params(LIMITS[2]),
            cost_estimate=cost(24 * span * KT * half, 6 << 20),
            name=f"middle_{chunk}",
        )(me, to_modes, from_modes, mode_depth, *operands)

    def to_rows(chunk, got, tables, prior):
        size = LANES + HALF
        more = prior is not None
        return pl.pallas_call(
            functools.partial(inverse_x, chunk, more=more),
            in_specs=[smem, vmem] + [anywhere] * (4 + more),
            out_specs=anywhere,
            out_shape=jax.ShapeDtypeStruct(state.shape, f32) if more else pltpu.HBM(state.shape, f32),
            scratch_shapes=[
                pltpu.VMEM(state.shape, f32),
                pltpu.VMEM((levels, 2, 2 * size, width), bf16),
                pltpu.VMEM((2, levels, HALF, width), f32),
                *[pltpu.VMEM((width, half), bf16)] * 4,
                pltpu.VMEM((devices * (STEP + STEP // 2), LANES), f32),
                pltpu.SemaphoreType.DMA((4 + levels,)),
                pltpu.SemaphoreType.DMA((levels - 1 + 2 * (half // TILE),)),
            ],
            compiler_params=params(LIMITS[3]),
            cost_estimate=cost(12 * width * levels * size * half, 8 << 20),
            name=f"inverse_x_{chunk}",
        )(place, got, *map(hbm, tables), *([hbm(prior)] if more else []))

    def exchange(sent):
        return lax.all_to_all(sent.reshape(-1, 1, LANES), AXES, 0, 0, tiled=True).reshape(sent.shape)

    sent = [to_columns(chunk) for chunk in range(chunks)]
    tables = all_tables(sent[-1])
    high, low = (a.reshape(2 * KT, half) for a in tables[4:])
    arrived = [exchange(part) for part in sent]
    returned = [exchange(through(chunk, got, high, low)) for chunk, got in enumerate(arrived)]
    value = None
    for chunk, got in enumerate(returned):
        value = to_rows(chunk, got, tables[:4], value)
    return value


def solution(mesh):
    placed = (P("lev", "wide", None), P(), P(), P())

    def shards(state, *rest):
        fits = packs(lax.axis_size("wide"), lax.axis_size("lev"), *state.shape)
        return (packed if fits else plain)(state, *rest)

    return jax.shard_map(
        shards, mesh=mesh, in_specs=placed, out_specs=P("lev", "wide", None), check_vma=False
    )
```
